128 devices in a mesh: sec: 2 (over core), blk: 64 (over x, y, z).
Axes of the slice: x: 4, y: 4, z: 4, core: 2. Of those that a mesh axis runs over, the one named last changes fastest.
Arguments:
- source: float32 [8192, 4096], P(('sec', 'blk')), may hold values from -6 to 6
- parent: int32 [1024], P(('sec', 'blk')), may hold values from -1 to 8191, as said below
- neighbor: int32 [1024, 6], P(('sec', 'blk')), may hold values from -1 to 1023, as said below
Outputs:
- solution: float32 [8192, 4096], P(('sec', 'blk'))
- residual: float32 [8192, 4096], P(('sec', 'blk'))
The draws below stay inside these ranges and needn't reach their ends.
Inputs may be any that keep to these rules, and one draw needn't show every extreme that they name: parent[g] is -1 for every family on sec index 1; a family on sec index 0 and blk index b names a block of a family on sec index 1 at blk index b or at blk index b + 1 (modulo the blk axis), exactly half of each device's families each way; no two families name the same block. neighbor[g, d] lies on the same index of sec as g, either on g's device or on the device whose blk index is g's minus (d = 0) or plus (d = 1) a quarter of the blk axis, minus (d = 2) or plus (d = 3) a sixteenth of it, minus (d = 4) or plus (d = 5) one; the relation is symmetric (if h is beside g in direction d, g is beside h in direction d xor 1); on each device at most 4 families have a neighbor on another device in direction -x, and likewise +x, at most 4 in -y and in +y, at most 4 in -z and in +z, and exactly so on some devices.
All inputs are finite; a program needn't handle non-finite values.
Results may differ from the reference program's by a relative error of at most 0.0001.
Values sent between devices are 32-bit elements; how exact they have to be, the bound alone decides.
No kernel may reach another device: no remote copies, remote signals or barrier semaphores. Data moves between devices by JAX's collectives and lax.ppermute only.
A program may use at most 128 MiB of HBM per device.

```python
import jax
import jax.numpy as jnp
from jax import lax

BS = 16
FX = 2
FY = 2
FZ = 2
NU = 3
ITERS = 2
FAM_DEV = 8
NB = 8192
N_SEC = 2
N_BLK = 64


def draw_source(key, part):
    first_key = jax.random.fold_in(key, 0)
    return jnp.clip(jax.random.normal(first_key, (NB, BS ** 3), jnp.float32), -6.0, 6.0)


def draw_parent(key, part):
    base = jax.random.fold_in(key, 11)
    split_key, place_key = jax.random.split(base)
    half = FAM_DEV // 2
    ranks = jax.vmap(lambda item: jax.random.permutation(item, FAM_DEV))(jax.random.split(split_key, N_BLK)).astype(jnp.int32)
    places = jax.vmap(lambda item: jax.random.permutation(item, 8 * FAM_DEV)[:FAM_DEV])(jax.random.split(place_key, N_BLK)).astype(jnp.int32)
    devices = jnp.arange(N_BLK, dtype=jnp.int32)[:, None]
    coarse_dev = jnp.where(ranks < half, devices, (devices + 1) % N_BLK)
    place = places[coarse_dev, ranks]
    fine = (N_BLK + coarse_dev) * (8 * FAM_DEV) + place
    coarse = jnp.full((N_BLK * FAM_DEV,), -1, jnp.int32)
    return jnp.concatenate([fine.reshape(-1).astype(jnp.int32), coarse])


def draw_neighbor(key, part):
    base = jax.random.fold_in(key, 23)
    depth = N_BLK // 16
    size_x, size_y, size_z = (4 * FX, 4 * FY, depth * FZ)
    index_x = jnp.arange(size_x, dtype=jnp.int32)[:, None, None]
    index_y = jnp.arange(size_y, dtype=jnp.int32)[None, :, None]
    index_z = jnp.arange(size_z, dtype=jnp.int32)[None, None, :]
    chip_cell = (index_x // FX * 4 + index_y // FY) * depth + index_z // FZ
    inner = (index_x % FX * FY + index_y % FY) * FZ + index_z % FZ
    result = jnp.full((N_SEC * N_BLK * FAM_DEV, 6), -1, jnp.int32)
    for section in range(N_SEC):
        local_key = jax.random.fold_in(base, section)
        local_order = jax.vmap(lambda item: jax.random.permutation(item, FAM_DEV))(jax.random.split(local_key, N_BLK)).astype(jnp.int32)
        local_index = local_order[chip_cell, inner]
        global_id = ((section * N_BLK + chip_cell) * FAM_DEV + local_index).astype(jnp.int32)
        padded = jnp.pad(global_id, 1, constant_values=-1)
        beside = jnp.stack([padded[:-2, 1:-1, 1:-1], padded[2:, 1:-1, 1:-1], padded[1:-1, :-2, 1:-1], padded[1:-1, 2:, 1:-1], padded[1:-1, 1:-1, :-2], padded[1:-1, 1:-1, 2:]], axis=-1)
        result = result.at[global_id.reshape(-1)].set(beside.reshape(-1, 6))
    return result


def setup_inputs(seed: int = 0) -> dict:
    keys = jax.random.split(jax.random.key(seed), 4)
    return {
        "source": draw_source(jax.random.fold_in(keys[3], 71), 0),
        "parent": draw_parent(jax.random.fold_in(keys[3], 71), 0),
        "neighbor": draw_neighbor(jax.random.fold_in(keys[3], 71), 0),
    }


DAMPING = 0.8
RESTRICT_WEIGHT = 0.5
OPPOSITE = (1, 0, 3, 2, 5, 4)


def to_family(blocks):
    total = blocks.shape[0] // 8
    cube = blocks.reshape(total, 2, 2, 2, BS, BS, BS)
    return cube.transpose(0, 1, 4, 2, 5, 3, 6).reshape(total, 2 * BS, 4 * BS * BS)


def to_blocks(family):
    total = family.shape[0]
    cube = family.reshape(total, 2, BS, 2, BS, 2, BS)
    return cube.transpose(0, 1, 3, 5, 2, 4, 6).reshape(total * 8, BS * BS * BS)


def faces_of(family):
    total, side_len = family.shape[0], family.shape[1]
    face_area = side_len * side_len
    return jnp.stack([family[:, 0], family[:, -1],
                      family[:, :, :side_len].reshape(total, face_area),
                      family[:, :, face_area - side_len:].reshape(total, face_area),
                      family[:, :, 0::side_len].reshape(total, face_area),
                      family[:, :, side_len - 1::side_len].reshape(total, face_area)], axis=1)


def apply_operator(family, halo_rows):
    total, side_len = family.shape[0], family.shape[1]
    lower_x = jnp.concatenate([halo_rows[:, 0:1], family[:, :-1]], axis=1)
    upper_x = jnp.concatenate([family[:, 1:], halo_rows[:, 1:2]], axis=1)
    lower_y = jnp.concatenate([halo_rows[:, 2].reshape(total, side_len, side_len), family[:, :, :-side_len]], axis=2)
    upper_y = jnp.concatenate([family[:, :, side_len:], halo_rows[:, 3].reshape(total, side_len, side_len)], axis=2)
    position = jnp.arange(side_len * side_len, dtype=jnp.int32) % side_len
    first_z = position == 0
    last_z = position == side_len - 1
    face_low = jnp.repeat(halo_rows[:, 4].reshape(total, side_len, side_len), side_len, axis=2)
    face_high = jnp.repeat(halo_rows[:, 5].reshape(total, side_len, side_len), side_len, axis=2)
    shifted_down = jnp.concatenate([jnp.zeros_like(family[:, :, :1]), family[:, :, :-1]], axis=2)
    shifted_up = jnp.concatenate([family[:, :, 1:], jnp.zeros_like(family[:, :, :1])], axis=2)
    lower_z = jnp.where(first_z, face_low, shifted_down)
    upper_z = jnp.where(last_z, face_high, shifted_up)
    return 6.0 * family - (lower_x + upper_x + lower_y + upper_y + lower_z + upper_z)


def restrict(family):
    total = family.shape[0]
    cube = family.reshape(total, BS, 2, BS, 2, BS, 2)
    return RESTRICT_WEIGHT * cube.sum(axis=(2, 4, 6)).reshape(total, BS * BS * BS)


def prolong(blocks):
    total = blocks.shape[0]
    cube = blocks.reshape(total, BS, 1, BS, 1, BS, 1)
    return jnp.broadcast_to(cube, (total, BS, 2, BS, 2, BS, 2)).reshape(total, 2 * BS, 4 * BS * BS)


def smooth(right_side):
    zero_halo = jnp.zeros((right_side.shape[0], 6, right_side.shape[2]), right_side.dtype)
    correction = (DAMPING / 6.0) * right_side
    for sweep_index in range(NU - 1):
        correction = correction + (DAMPING / 6.0) * (right_side - apply_operator(correction, zero_halo))
    return correction


def halo_faces(family, neighbor):
    face_table = faces_of(family)
    face_area = face_table.shape[2]
    flat_table = face_table.reshape(-1, face_area)
    opposite = jnp.array(OPPOSITE, dtype=jnp.int32)
    wanted = jnp.maximum(neighbor, 0) * 6 + opposite[None, :]
    picked = jnp.take(flat_table, wanted.reshape(-1), axis=0).reshape(neighbor.shape[0], 6, face_area)
    return jnp.where((neighbor >= 0)[:, :, None], picked, 0.0)


def grouped(function, arrays):
    groups = arrays[0].shape[0] // FAM_DEV
    shaped = tuple(item.reshape((groups, FAM_DEV) + item.shape[1:]) for item in arrays)
    result = lax.map(function, shaped)
    return result.reshape((groups * FAM_DEV,) + result.shape[2:])


def residual_of(source_fam, solution, neighbor):
    halo_rows = halo_faces(solution, neighbor)

    def one_group(packed):
        return packed[0] - apply_operator(packed[1], packed[2])

    return grouped(one_group, (source_fam, solution, halo_rows))


def smooth_group(packed):
    return smooth(packed[0])


def reference(source, parent, neighbor):
    source_fam = to_family(source)
    solution = jnp.zeros_like(source_fam)
    has_parent = parent >= 0
    block_total = source.shape[0]
    target = jnp.where(has_parent, parent, block_total).astype(jnp.int32)
    lookup = jnp.maximum(parent, 0).astype(jnp.int32)
    for iteration in range(ITERS):
        residue = residual_of(source_fam, solution, neighbor)
        down_blocks = restrict(residue)
        right_blocks = to_blocks(residue).at[target].add(down_blocks, mode="drop")
        correction = grouped(smooth_group, (to_family(right_blocks),))
        lifted = jnp.where(has_parent[:, None], jnp.take(to_blocks(correction), lookup, axis=0), 0.0)
        solution = solution + correction + prolong(lifted)
    residue = residual_of(source_fam, solution, neighbor)
    return to_blocks(solution), to_blocks(residue)
```

```python
import jax
import jax.numpy as jnp
from jax import lax
from jax.experimental import pallas as pl
from jax.experimental.pallas import tpu as pltpu
from jax.sharding import PartitionSpec as P

AX = ("sec", "blk")
N_BLK = 64
FAM = 8
WEIGHT = 0.8 / 6.0
PAD_ROWS = 34 * 64
F32 = jnp.float32
VMEM = pl.BlockSpec(memory_space=pltpu.VMEM)
SMEM = pl.BlockSpec(memory_space=pltpu.SMEM)


def swap_pairs(unit, color):
    pairs, used = [], set()
    for b in range(N_BLK - unit):
        if (b // unit) % 2 == color:
            for s in (0, N_BLK):
                pairs += [(s + b, s + b + unit), (s + b + unit, s + b)]
            used |= {b, b + unit}
    for b in range(N_BLK):
        if b not in used:
            pairs += [(b, N_BLK + b), (N_BLK + b, b)]
    return pairs


def level_pairs(step):
    pairs = []
    for b in range(N_BLK):
        c = N_BLK + (b + step) % N_BLK
        pairs += [(b, c), (c, b)]
    return pairs


UNITS = (16, 4, 1)
HALO_PAIRS = [swap_pairs(unit, color) for unit in UNITS for color in (0, 1)]
OWN_PAIRS = level_pairs(0)
NEXT_PAIRS = level_pairs(1)


def swap(x, pairs):
    return lax.ppermute(x, AX, pairs)


def position():
    return lax.axis_index("sec"), lax.axis_index("blk")


def parities(blk):
    return [(blk >> 4) & 1, (blk >> 2) & 1, blk & 1]


def lane_parts():
    lane = lax.broadcasted_iota(jnp.int32, (8, 128), 1)
    return lane >> 4, lane & 15


def roll(x, by):
    return pltpu.roll(x, by, 1)


def rows(ref, start, size=8):
    return ref[pl.ds(pl.multiple_of(start, 8), size), :]


def put(ref, start, value):
    ref[pl.ds(pl.multiple_of(start, 8), value.shape[0]), :] = value


def plane(ref, x):
    base = (x + 1) * 64
    return [[rows(ref, base + (q * 2 + oz) * 8) for oz in range(2)] for q in range(4)]


def around(a, below, above, ylo, z, hy=None, hz=None):
    zero = jnp.zeros((8, 128), F32)
    if hy is None:
        hy = [[zero, zero], [zero, zero]]
    if hz is None:
        hz = [[zero, zero] for _ in range(4)]
    y_first, y_last = ylo == 0, ylo == 7
    z_first, z_last = z == 0, z == 15
    down = [[roll(a[q][o], 16) for o in range(2)] for q in range(4)]
    up = [[roll(a[q][o], 112) for o in range(2)] for q in range(4)]
    total = []
    for q in range(4):
        line = []
        for o in range(2):
            low_y = jnp.where(y_first, down[q - 1][o] if q else hy[0][o], down[q][o])
            high_y = jnp.where(y_last, up[q + 1][o] if q < 3 else hy[1][o], up[q][o])
            if o == 0:
                low_z = jnp.where(z_first, hz[q][0], roll(a[q][0], 1))
                high_z = roll(jnp.where(z_first, down[q][1], a[q][0]), 127)
            else:
                low_z = roll(jnp.where(z_last, up[q][0], a[q][1]), 1)
                high_z = jnp.where(z_last, hz[q][1], roll(a[q][1], 127))
            line.append((low_y + high_y) + (low_z + high_z) + (below[q][o] + above[q][o]))
        total.append(line)
    return total


def clear_pads(ref):
    for start in (0, 33 * 64):
        ref[start : start + 64, :] = jnp.zeros((64, 128), F32)


def smooth(rhs, mid, emit):
    ylo, z = lane_parts()
    clear_pads(rhs)
    clear_pads(mid)

    def first(x, _):
        a = plane(rhs, x)
        m = around(a, plane(rhs, x - 1), plane(rhs, x + 1), ylo, z)
        for q in range(4):
            for o in range(2):
                put(mid, (x + 1) * 64 + (q * 2 + o) * 8, 1.2 * a[q][o] + WEIGHT * m[q][o])
        return 0

    def second(x, _):
        a = plane(mid, x)
        m = around(a, plane(mid, x - 1), plane(mid, x + 1), ylo, z)
        for q in range(4):
            for o in range(2):
                at = (x + 1) * 64 + (q * 2 + o) * 8
                emit(at, WEIGHT * (rows(rhs, at) + 0.2 * a[q][o] + WEIGHT * m[q][o]))
        return 0

    lax.fori_loop(0, 32, first, 0)
    lax.fori_loop(0, 32, second, 0)


def restrict_pair(p, i, ylo, z, down):
    z_even, y_even = (z & 1) == 0, (ylo & 1) == 0
    index = (2 * (ylo & 3) + (ylo >> 2)) * 16 + 2 * (z & 7) + (z >> 3)
    for oy in range(2):
        u = []
        for a in range(2):
            lo, hi = p[2 * oy + a]
            u.append(jnp.where(z_even, lo + roll(lo, 127), hi + roll(hi, 1)))
        m = jnp.where(y_even, u[0] + roll(u[0], 112), u[1] + roll(u[1], 16))
        put(down, (oy * 16 + i) * 8, 0.5 * jnp.take_along_axis(m, index, axis=1))


def parent_slots(parent, blk):
    own_count, next_count = jnp.int32(0), jnp.int32(0)
    found = []
    for g in range(FAM):
        value = parent[g]
        chip = (value >> 6) - N_BLK
        to_own = (value >= 0) & (chip == blk)
        to_next = (value >= 0) & (chip == ((blk + 1) & (N_BLK - 1)))
        found.append((to_own, to_next, own_count, next_count, value & 63))
        own_count = own_count + to_own.astype(jnp.int32)
        next_count = next_count + to_next.astype(jnp.int32)
    return found


def send_down(down, parent, blk, own, nxt, tags):
    for buf in (own, nxt):
        if tags:
            buf[128:136, :] = jnp.full((8, 128), -1.0, F32)
    for g, (to_own, to_next, own_slot, next_slot, block) in enumerate(parent_slots(parent, blk)):
        for going, slot, buf in ((to_own, own_slot, own), (to_next, next_slot, nxt)):

            @pl.when(going)
            def _(slot=slot, buf=buf, block=block, g=g):
                put(buf, slot * 32, down[pl.ds(g, 32, stride=8), :])
                if tags:
                    buf[pl.ds(128 + slot, 1), :] = jnp.full((1, 128), block.astype(F32), F32)


def block_start(block):
    f, o = block >> 3, block & 7
    return ((o >> 2) * 16 + 1) * 64 + (((o >> 1) & 1) * 4 + (o & 1)) * 8 + f


def add_incoming(rhs, tags, arrived):
    for j in range(8):
        buf, slot, tag = arrived[j // 4], j % 4, tags[j]

        @pl.when(tag >= 0)
        def _(buf=buf, slot=slot, tag=tag):
            start = block_start(tag)
            for yh in range(2):
                at = pl.ds(start + yh * 16, 16, stride=64)
                rhs[at, :] = rhs[at, :] + buf[slot * 32 + yh * 16 : slot * 32 + yh * 16 + 16, :]


def answer(correction, tags, out):
    for j in range(8):
        buf, slot, tag = out[j // 4], j % 4, tags[j]

        @pl.when(tag >= 0)
        def _(buf=buf, slot=slot, tag=tag):
            start = block_start(tag)
            for yh in range(2):
                buf[slot * 32 + yh * 16 : slot * 32 + yh * 16 + 16, :] = correction[
                    pl.ds(start + yh * 16, 16, stride=64), :
                ]


def first_down_kernel(parent, source, own, nxt, down):
    sec, blk = position()
    ylo, z = lane_parts()

    @pl.when(sec == 0)
    def _():
        def pair(i, _):
            x = (2 * i) & 15
            ox4 = (i >> 3) * 4
            p = []
            for q in range(4):
                line = []
                for oz in range(2):
                    o = ox4 + (q // 2) * 2 + oz
                    c = x * 2 + q % 2
                    line.append(
                        source[pl.ds(c * 8 + o, 8, stride=256), :]
                        + source[pl.ds((c + 2) * 8 + o, 8, stride=256), :]
                    )
                p.append(line)
            restrict_pair(p, i, ylo, z, down)
            return 0

        lax.fori_loop(0, 16, pair, 0)
        send_down(down, parent, blk, own, nxt, True)


def load_kernel(source, src, sol, mid):
    sec, _ = position()

    def copy(x, _):
        for ox in range(2):
            for q in range(4):
                for oz in range(2):
                    o = ox * 4 + (q // 2) * 2 + oz
                    c = x * 2 + q % 2
                    put(src, (ox * 16 + x + 1) * 64 + (q * 2 + oz) * 8, source[pl.ds(c * 8 + o, 8, stride=256), :])
        return 0

    lax.fori_loop(0, 16, copy, 0)

    @pl.when(sec == 0)
    def _():
        def emit(at, value):
            put(sol, at, value)

        smooth(src, mid, emit)


def coarse_kernel(first, *refs):
    if first:
        res, sol, in_own, in_next, out_sol, out_own, out_next, tags, rhs, mid, smem, sem = refs
    else:
        tags, res, sol, in_own, in_next, out_sol, out_own, out_next, rhs, mid, corr = refs
    sec, _ = position()

    if first:
        for j in range(8):
            tags[j] = jnp.int32(-1)

    @pl.when(sec == 0)
    def _():
        def copy(i, _):
            put(out_sol, i * 64, rows(sol, i * 64, 64))
            return 0

        lax.fori_loop(1, 33, copy, 0)

    @pl.when(sec == 1)
    def _():
        if first:
            copies = [
                pltpu.make_async_copy(buf.at[128:136, :], smem.at[k], sem.at[k])
                for k, buf in enumerate((in_own, in_next))
            ]
            for c in copies:
                c.start()

        def copy(i, _):
            put(rhs, i * 64, rows(res, i * 64, 64))
            return 0

        lax.fori_loop(1, 33, copy, 0)
        if first:
            for k, c in enumerate(copies):
                c.wait()
                for j in range(4):
                    tags[k * 4 + j] = smem[k, j, 0].astype(jnp.int32)
        add_incoming(rhs, tags, (in_own, in_next))

        def emit(at, value):
            if first:
                put(out_sol, at, value)
            else:
                put(corr, at, value)
                put(out_sol, at, rows(sol, at) + value)

        smooth(rhs, mid, emit)
        answer(out_sol if first else corr, tags, (out_own, out_next))


def lift_kernel(parent, sol, in_own, in_next, out_sol, *refs):
    out, (lift, face) = refs[:6], refs[6:]
    sec, blk = position()
    ylo, z = lane_parts()

    @pl.when(sec == 1)
    def _():
        def copy(i, _):
            put(out_sol, i * 64, rows(sol, i * 64, 64))
            return 0

        lax.fori_loop(1, 33, copy, 0)

    @pl.when(sec == 0)
    def _():
        for g, (to_own, to_next, own_slot, next_slot, _) in enumerate(parent_slots(parent, blk)):
            at = pl.ds(g, 32, stride=8)

            @pl.when(to_own)
            def _(at=at, slot=own_slot):
                lift[at, :] = rows(in_own, slot * 32, 32)

            @pl.when(to_next)
            def _(at=at, slot=next_slot):
                lift[at, :] = rows(in_next, slot * 32, 32)

            @pl.when(jnp.logical_not(to_own | to_next))
            def _(at=at):
                lift[at, :] = jnp.zeros((32, 128), F32)

        index = [[(4 * a + (ylo >> 1)) * 16 + 8 * b + (z >> 1) for b in range(2)] for a in range(2)]

        def add(i, _):
            for oy in range(2):
                value = rows(lift, (oy * 16 + i) * 8)
                for a in range(2):
                    for b in range(2):
                        wide = jnp.take_along_axis(value, index[a][b], axis=1)
                        for x in range(2):
                            at = (2 * i + x + 1) * 64 + ((2 * oy + a) * 2 + b) * 8
                            put(out_sol, at, rows(sol, at) + wide)
            return 0

        lax.fori_loop(0, 16, add, 0)

    put(face, 0, rows(out_sol, 64, 64))
    put(face, 64, rows(out_sol, 32 * 64, 64))

    def pack(x, _):
        base = (x + 1) * 64
        y_at, z_at = x & 7, x & 15
        y_mask, z_mask = ylo == y_at, z == z_at
        for oz in range(2):
            at = (oz * 4 + (x >> 3)) * 8
            low = roll(rows(out_sol, base + oz * 8), 16 * y_at)
            high = roll(rows(out_sol, base + (6 + oz) * 8), (16 * y_at + 16) & 127)
            put(face, 128 + at, jnp.where(y_mask, low, rows(face, 128 + at)))
            put(face, 192 + at, jnp.where(y_mask, high, rows(face, 192 + at)))
        for q in range(4):
            at = (q * 2 + (x >> 4)) * 8
            low = roll(rows(out_sol, base + q * 16), z_at)
            high = roll(rows(out_sol, base + q * 16 + 8), (z_at + 113) & 127)
            put(face, 256 + at, jnp.where(z_mask, low, rows(face, 256 + at)))
            put(face, 320 + at, jnp.where(z_mask, high, rows(face, 320 + at)))
        return 0

    lax.fori_loop(0, 32, pack, 0)
    for axis, parity in enumerate(parities(blk)):
        for color in range(2):
            d = 2 * axis + (parity == color).astype(jnp.int32)
            out[2 * axis + color][...] = rows(face, d * 64, 64)


def residual_kernel(last, parent, neighbor, src, sol, *refs):
    sent, got = refs[:6], refs[6:12]
    if last:
        res, halo, table = refs[12:]
    else:
        res, own, nxt, halo, table, down = refs[12:]
    sec, blk = position()
    ylo, z = lane_parts()

    for axis, parity in enumerate(parities(blk)):
        for color in range(2):
            odd = (parity == color).astype(jnp.int32)
            put(table, (2 * axis + 1 - odd) * 128, sent[2 * axis + color][...])
            put(table, (2 * axis + odd) * 128 + 64, got[2 * axis + color][...])
    device = sec * N_BLK + blk

    def gather(g, _):
        for d in range(6):
            other = neighbor[g, d]
            local = (other >> 3) == device
            start = d * 128 + jnp.where(local, 0, 64) + (other & 7)
            value = table[pl.ds(start, 8, stride=8), :]
            halo[pl.ds(d * 64 + g, 8, stride=8), :] = jnp.where(other >= 0, value, 0.0)
        return 0

    lax.fori_loop(0, FAM, gather, 0)

    def side(base):
        return [[rows(halo, base + (q * 2 + o) * 8) for o in range(2)] for q in range(4)]

    def residue(x, below, above):
        a = plane(sol, x)
        y_at, z_at = x & 7, x & 15
        y_rows = [128 + (o * 4 + (x >> 3)) * 8 for o in range(2)]
        hy = [
            [roll(rows(halo, y_rows[o]), (128 - 16 * y_at) & 127) for o in range(2)],
            [roll(rows(halo, y_rows[o] + 64), 112 - 16 * y_at) for o in range(2)],
        ]
        hz = []
        for q in range(4):
            at = 256 + (q * 2 + (x >> 4)) * 8
            hz.append([roll(rows(halo, at), (128 - z_at) & 127), roll(rows(halo, at + 64), 15 - z_at)])
        m = around(a, below, above, ylo, z, hy, hz)
        s = plane(src, x)
        return [[s[q][o] - 6.0 * a[q][o] + m[q][o] for o in range(2)] for q in range(4)]

    def store(x, r):
        if last:
            for q in range(4):
                for o in range(2):
                    octant = (x >> 4) * 4 + (q // 2) * 2 + o
                    c = (x & 15) * 2 + q % 2
                    res[pl.ds(c * 8 + octant, 8, stride=256), :] = r[q][o]
        else:
            for q in range(4):
                for o in range(2):
                    put(res, (x + 1) * 64 + (q * 2 + o) * 8, r[q][o])

    def pair(i, _, low=None, high=None):
        x = 2 * i
        r0 = residue(x, plane(sol, x - 1) if low is None else low, plane(sol, x + 1))
        r1 = residue(x + 1, plane(sol, x), plane(sol, x + 2) if high is None else high)
        store(x, r0)
        store(x + 1, r1)
        if not last:

            @pl.when(sec == 0)
            def _():
                p = [[r0[q][o] + r1[q][o] for o in range(2)] for q in range(4)]
                restrict_pair(p, i, ylo, z, down)

        return 0

    pair(0, 0, low=side(0))
    lax.fori_loop(1, 15, pair, 0)
    pair(15, 0, high=side(64))
    if not last:

        @pl.when(sec == 0)
        def _():
            send_down(down, parent, blk, own, nxt, False)


def fine_kernel(res, sol, out_sol, rhs, mid):
    sec, _ = position()

    @pl.when(sec == 1)
    def _():
        def copy(i, _):
            put(out_sol, i * 64, rows(sol, i * 64, 64))
            return 0

        lax.fori_loop(1, 33, copy, 0)

    @pl.when(sec == 0)
    def _():
        def copy(i, _):
            put(rhs, i * 64, rows(res, i * 64, 64))
            return 0

        lax.fori_loop(1, 33, copy, 0)

        def emit(at, value):
            put(out_sol, at, rows(sol, at) + value)

        smooth(rhs, mid, emit)


def unload_kernel(sol, out):
    def copy(x, _):
        for ox in range(2):
            for q in range(4):
                for oz in range(2):
                    o = ox * 4 + (q // 2) * 2 + oz
                    c = x * 2 + q % 2
                    out[pl.ds(c * 8 + o, 8, stride=256), :] = rows(sol, (ox * 16 + x + 1) * 64 + (q * 2 + oz) * 8)
        return 0

    lax.fori_loop(0, 16, copy, 0)


def shape(n, dtype=F32):
    return jax.ShapeDtypeStruct((n, 128), dtype)


def scratch(n):
    return pltpu.VMEM((n, 128), F32)


def call(kernel, name, in_specs, out_shape, scratch_shapes=(), out_specs=None):
    return pl.pallas_call(
        kernel,
        name=name,
        in_specs=in_specs,
        out_shape=out_shape,
        out_specs=out_specs or [VMEM] * len(out_shape),
        scratch_shapes=list(scratch_shapes),
        compiler_params=pltpu.CompilerParams(vmem_limit_bytes=32 << 20),
    )


def local(source, parent, neighbor):
    tiles = source.reshape(FAM, 8, 32, 128).transpose(0, 2, 1, 3).reshape(2048, 128)
    pad, pads = shape(PAD_ROWS), scratch(PAD_ROWS)

    def both(own, nxt):
        return swap(nxt, NEXT_PAIRS), swap(own, OWN_PAIRS)

    own, nxt = call(first_down_kernel, "first_down", [SMEM, VMEM], (shape(136), shape(136)), [scratch(256)])(
        parent, tiles
    )
    got_next, got_own = both(own, nxt)
    src, sol = call(load_kernel, "load", [VMEM], (pad, pad), [pads])(tiles)
    res, tags = src, None
    for iteration in range(2):
        first = iteration == 0
        if first:
            sol, own, nxt, tags = call(
                lambda *refs: coarse_kernel(True, *refs),
                "coarse_0",
                [VMEM] * 4,
                (pad, shape(128), shape(128), jax.ShapeDtypeStruct((8,), jnp.int32)),
                [pads, pads, pltpu.SMEM((2, 8, 128), F32), pltpu.SemaphoreType.DMA((2,))],
                [VMEM, VMEM, VMEM, SMEM],
            )(res, sol, got_own, got_next)
        else:
            sol, own, nxt = call(
                lambda *refs: coarse_kernel(False, *refs),
                "coarse_1",
                [SMEM] + [VMEM] * 4,
                (pad, shape(128), shape(128)),
                [pads, pads, pads],
            )(tags, res, sol, got_own, got_next)
        got_next, got_own = both(own, nxt)
        out = call(
            lift_kernel,
            f"lift_{iteration}",
            [SMEM, VMEM, VMEM, VMEM],
            (pad,) + (shape(64),) * 6,
            [scratch(256), scratch(384)],
        )(parent, sol, got_own, got_next)
        sol, sent = out[0], out[1:]
        got = [swap(s, pairs) for s, pairs in zip(sent, HALO_PAIRS)]
        ins = [SMEM, SMEM] + [VMEM] * 14
        if first:
            res, own, nxt = call(
                lambda *refs: residual_kernel(False, *refs),
                "residual_0",
                ins,
                (pad, shape(128), shape(128)),
                [scratch(384), scratch(768), scratch(256)],
            )(parent, neighbor, src, sol, *sent, *got)
            got_next, got_own = both(own, nxt)
            (sol,) = call(fine_kernel, "fine", [VMEM, VMEM], (pad,), [pads, pads])(res, sol)
        else:
            (solution,) = call(unload_kernel, "unload", [VMEM], (shape(2048),))(sol)
            (residual,) = call(
                lambda *refs: residual_kernel(True, *refs),
                "residual_1",
                ins,
                (shape(2048),),
                [scratch(384), scratch(768)],
            )(parent, neighbor, src, sol, *sent, *got)

    def blocks(x):
        return x.reshape(FAM, 32, 8, 128).transpose(0, 2, 1, 3).reshape(64, 4096)

    return blocks(solution), blocks(residual)


def solution(mesh):
    return jax.shard_map(
        local,
        mesh=mesh,
        in_specs=(P(AX, None), P(AX), P(AX, None)),
        out_specs=(P(AX, None), P(AX, None)),
        check_vma=False,
    )
```

```python
import functools

import jax
import jax.numpy as jnp
from jax import lax
from jax.experimental import pallas as pl
from jax.experimental.pallas import tpu as pltpu
from jax.sharding import PartitionSpec as P

AX = ("sec", "blk")
N_BLK = 64
FAM = 8
WEIGHT = 0.8 / 6.0
PAD_ROWS = 34 * 64
GROUP = 4
F32 = jnp.float32
VMEM = pl.BlockSpec(memory_space=pltpu.VMEM)
SMEM = pl.BlockSpec(memory_space=pltpu.SMEM)


def swap_pairs(unit, color):
    pairs, used = [], set()
    for b in range(N_BLK - unit):
        if (b // unit) % 2 == color:
            for s in (0, N_BLK):
                pairs += [(s + b, s + b + unit), (s + b + unit, s + b)]
            used |= {b, b + unit}
    for b in range(N_BLK):
        if b not in used:
            pairs += [(b, N_BLK + b), (N_BLK + b, b)]
    return pairs


def level_pairs(step):
    pairs = []
    for b in range(N_BLK):
        c = N_BLK + (b + step) % N_BLK
        pairs += [(b, c), (c, b)]
    return pairs


UNITS = (16, 4, 1)
HALO_PAIRS = [swap_pairs(unit, color) for unit in UNITS for color in (0, 1)]
OWN_PAIRS = level_pairs(0)
NEXT_PAIRS = level_pairs(1)


def swap(x, pairs):
    return lax.ppermute(x, AX, pairs)


def position():
    return lax.axis_index("sec"), lax.axis_index("blk")


def parities(blk):
    return [(blk >> 4) & 1, (blk >> 2) & 1, blk & 1]


def lane_parts():
    lane = lax.broadcasted_iota(jnp.int32, (8, 128), 1)
    return lane >> 4, lane & 15


def roll(x, by):
    return pltpu.roll(x, by, 1)


def rows(ref, start, size=8):
    return ref[pl.ds(pl.multiple_of(start, 8), size), :]


def put(ref, start, value):
    ref[pl.ds(pl.multiple_of(start, 8), value.shape[0]), :] = value


def plane(ref, x):
    base = (x + 1) * 64
    return [[rows(ref, base + (q * 2 + oz) * 8) for oz in range(2)] for q in range(4)]


def around(a, below, above, j, k, hy=None, hz=None):
    zero = jnp.zeros((8, 128), F32)
    if hy is None:
        hy = [[zero, zero], [zero, zero]]
    if hz is None:
        hz = [[zero, zero] for _ in range(4)]
    y_low = [jnp.where(j == 0, hy[0][p], roll(a[3][p], 16)) for p in range(2)]
    y_high = [jnp.where(j == 7, hy[1][p], roll(a[0][p], 112)) for p in range(2)]
    total = []
    for r in range(4):
        z_low = jnp.where(k == 0, hz[r][0], roll(a[r][1], 1))
        z_high = jnp.where(k == 15, hz[r][1], roll(a[r][0], 127))
        line = []
        for p in range(2):
            y_sum = (a[r - 1][p] if r else y_low[p]) + (a[r + 1][p] if r < 3 else y_high[p])
            z_sum = a[r][1 - p] + (z_high if p else z_low)
            line.append((y_sum + z_sum) + (below[r][p] + above[r][p]))
        total.append(line)
    return total


def exchange(a, b, bit, shift):
    return jnp.where(bit, roll(b, shift), a), jnp.where(bit, b, roll(a, 128 - shift))


def spread_index(j, k):
    return ((j & 1) * 4 + (j >> 1)) * 16 + 2 * (k & 7) + (k >> 3)


def to_working(v, j, k):
    s = [exchange(v[q][0], v[q][1], (k & 1) == 1, 1) for q in range(4)]
    index = spread_index(j, k)
    result = [[None, None] for _ in range(4)]
    for p in range(2):
        t = [exchange(s[2 * h][p], s[2 * h + 1][p], (j & 1) == 1, 16) for h in range(2)]
        for low in range(2):
            pair = exchange(t[0][low], t[1][low], (j & 2) == 2, 32)
            for high in range(2):
                result[low + 2 * high][p] = jnp.take_along_axis(pair[high], index, axis=1)
    return result


def to_given(a, j, k):
    index = (2 * (j & 3) + (j >> 2)) * 16 + (k >> 1) + 8 * (k & 1)
    s = [[None, None] for _ in range(4)]
    for p in range(2):
        t = [[None, None], [None, None]]
        for low in range(2):
            pair = [jnp.take_along_axis(a[low + 2 * high][p], index, axis=1) for high in range(2)]
            t[0][low], t[1][low] = exchange(pair[0], pair[1], (j & 2) == 2, 32)
        for h in range(2):
            s[2 * h][p], s[2 * h + 1][p] = exchange(t[h][0], t[h][1], (j & 1) == 1, 16)
    return [exchange(s[q][0], s[q][1], (k & 1) == 1, 1) for q in range(4)]


def given_rows(x, q, oz):
    octant = (x >> 4) * 4 + (q // 2) * 2 + oz
    return pl.ds(((x & 15) * 2 + q % 2) * 8 + octant, 8, stride=256)


def given_plane(ref, x):
    return [[ref[given_rows(x, q, oz), :] for oz in range(2)] for q in range(4)]


def put_given(ref, x, v):
    for q in range(4):
        for oz in range(2):
            ref[given_rows(x, q, oz), :] = v[q][oz]


def put_plane(ref, x, a):
    for r in range(4):
        for p in range(2):
            put(ref, (x + 1) * 64 + (r * 2 + p) * 8, a[r][p])


def clear_pads(ref):
    for start in (0, 33 * 64):
        ref[start : start + 64, :] = jnp.zeros((64, 128), F32)


def smooth(rhs, mid, emit):
    j, k = lane_parts()
    clear_pads(rhs)
    clear_pads(mid)

    def sweep(src, write):
        def body(i, _):
            x0 = i * GROUP
            p = [plane(src, x0 + m - 1) for m in range(GROUP + 2)]
            result = [around(p[m + 1], p[m], p[m + 2], j, k) for m in range(GROUP)]
            for m in range(GROUP):
                for r in range(4):
                    for c in range(2):
                        write((x0 + m + 1) * 64 + (r * 2 + c) * 8, p[m + 1][r][c], result[m][r][c])
            return 0

        lax.fori_loop(0, 32 // GROUP, body, 0)

    def first(at, a, m):
        put(mid, at, 1.2 * a + WEIGHT * m)

    def second(at, a, m):
        emit(at, WEIGHT * (rows(rhs, at) + 0.2 * a + WEIGHT * m))

    sweep(rhs, first)
    sweep(mid, second)


def put_down(down, i, pair):
    for r in range(2):
        put(down, (r * 16 + i) * 8, pair[r])


def restrict_pair(a, b):
    c = [[a[r][p] + b[r][p] for p in range(2)] for r in range(4)]
    return [0.5 * ((c[2 * r][0] + c[2 * r][1]) + (c[2 * r + 1][0] + c[2 * r + 1][1])) for r in range(2)]


def restrict_given(a, b, j, k):
    z_even, y_even, high = (k & 1) == 0, (j & 1) == 0, (j & 2) == 2
    u = []
    for q in range(4):
        lo, hi = a[q][0] + b[q][0], a[q][1] + b[q][1]
        u.append(jnp.where(z_even, lo + roll(lo, 127), hi + roll(hi, 1)))
    m = []
    for h in range(2):
        m.append(jnp.where(y_even, u[2 * h] + roll(u[2 * h], 112), u[2 * h + 1] + roll(u[2 * h + 1], 16)))
    index = spread_index(j, k)
    return [0.5 * jnp.take_along_axis(n, index, axis=1) for n in exchange(m[0], m[1], high, 32)]


def parent_slots(parent, blk):
    own_count, next_count = jnp.int32(0), jnp.int32(0)
    found = []
    for g in range(FAM):
        value = parent[g]
        chip = (value >> 6) - N_BLK
        to_own = (value >= 0) & (chip == blk)
        to_next = (value >= 0) & (chip == ((blk + 1) & (N_BLK - 1)))
        found.append((to_own, to_next, own_count, next_count, value & 63))
        own_count = own_count + to_own.astype(jnp.int32)
        next_count = next_count + to_next.astype(jnp.int32)
    return found


def send_down(down, parent, blk, own, nxt, tags):
    for buf in (own, nxt):
        if tags:
            buf[128:136, :] = jnp.full((8, 128), -1.0, F32)
    for g, (to_own, to_next, own_slot, next_slot, block) in enumerate(parent_slots(parent, blk)):
        for going, slot, buf in ((to_own, own_slot, own), (to_next, next_slot, nxt)):

            @pl.when(going)
            def _(slot=slot, buf=buf, block=block, g=g):
                put(buf, slot * 32, down[pl.ds(g, 32, stride=8), :])
                if tags:
                    buf[pl.ds(128 + slot, 1), :] = jnp.full((1, 128), block.astype(F32), F32)


def block_place(block, s, half):
    f, o = block >> 3, block & 7
    start = ((o >> 2) * 16 + 8 * half + 1) * 64 + f
    at = [[pl.ds(start + ((2 * t + s) * 2 + p) * 8, 8, stride=64) for p in range(2)] for t in range(2)]
    return at, (o >> 1) & 1, o & 1


def add_incoming(rhs, tags, arrived):
    j, k = lane_parts()
    index = [[(2 * (j & 3) + t) * 16 + 2 * (k & 7) + p for p in range(2)] for t in range(2)]
    for n in range(8):
        buf, slot, tag = arrived[n // 4], n % 4, tags[n]

        @pl.when(tag >= 0)
        def _(buf=buf, slot=slot, tag=tag):
            for s in range(2):
                for half in range(2):
                    at, oy, oz = block_place(tag, s, half)
                    here = ((j >> 2) == oy) & ((k >> 3) == oz)
                    value = rows(buf, slot * 32 + s * 16 + half * 8)
                    for t in range(2):
                        for p in range(2):
                            spread = jnp.take_along_axis(value, index[t][p], axis=1)
                            rhs[at[t][p], :] = rhs[at[t][p], :] + jnp.where(here, spread, 0.0)


def answer(correction, tags, out):
    j, k = lane_parts()
    y_odd, z_odd = (j & 1) == 1, (k & 1) == 1
    for n in range(8):
        buf, slot, tag = out[n // 4], n % 4, tags[n]

        @pl.when(tag >= 0)
        def _(buf=buf, slot=slot, tag=tag):
            for s in range(2):
                for half in range(2):
                    at, oy, oz = block_place(tag, s, half)
                    index = (4 * oy + (j >> 1)) * 16 + 8 * oz + (k >> 1)
                    v = [
                        [jnp.take_along_axis(correction[at[t][p], :], index, axis=1) for p in range(2)]
                        for t in range(2)
                    ]
                    v = [jnp.where(z_odd, v[t][1], v[t][0]) for t in range(2)]
                    put(buf, slot * 32 + s * 16 + half * 8, jnp.where(y_odd, v[1], v[0]))


def first_down_kernel(parent, source, own, nxt, down):
    sec, blk = position()
    j, k = lane_parts()

    @pl.when(sec == 0)
    def _():
        def pair(i):
            return restrict_given(given_plane(source, 2 * i), given_plane(source, 2 * i + 1), j, k)

        def pairs(n, _):
            done = [pair(4 * n + m) for m in range(4)]
            for m in range(4):
                put_down(down, 4 * n + m, done[m])
            return 0

        lax.fori_loop(0, 4, pairs, 0)
        send_down(down, parent, blk, own, nxt, True)


def load_kernel(source, src, sol, mid):
    sec, _ = position()

    j, k = lane_parts()

    def convert(i, _):
        planes = [to_working(given_plane(source, GROUP * i + m), j, k) for m in range(GROUP)]
        for m in range(GROUP):
            put_plane(src, GROUP * i + m, planes[m])
        return 0

    lax.fori_loop(0, 32 // GROUP, convert, 0)

    @pl.when(sec == 0)
    def _():
        def emit(at, value):
            put(sol, at, value)

        smooth(src, mid, emit)


def coarse_kernel(first, *refs):
    if first:
        res, sol, in_own, in_next, out_sol, out_own, out_next, tags, rhs, mid, smem, sem = refs
    else:
        tags, res, sol, in_own, in_next, out_sol, out_own, out_next, rhs, mid, corr = refs
    sec, _ = position()

    if first:
        for j in range(8):
            tags[j] = jnp.int32(-1)

    @pl.when(sec == 0)
    def _():
        def copy(i, _):
            put(out_sol, i * 64, rows(sol, i * 64, 64))
            return 0

        lax.fori_loop(1, 33, copy, 0)

    @pl.when(sec == 1)
    def _():
        if first:
            copies = [
                pltpu.make_async_copy(buf.at[128:136, :], smem.at[k], sem.at[k])
                for k, buf in enumerate((in_own, in_next))
            ]
            for c in copies:
                c.start()

        def copy(i, _):
            put(rhs, i * 64, rows(res, i * 64, 64))
            return 0

        lax.fori_loop(1, 33, copy, 0)
        if first:
            for k, c in enumerate(copies):
                c.wait()
                for j in range(4):
                    tags[k * 4 + j] = smem[k, j, 0].astype(jnp.int32)
        add_incoming(rhs, tags, (in_own, in_next))

        def emit(at, value):
            if first:
                put(out_sol, at, value)
            else:
                put(corr, at, value)
                put(out_sol, at, rows(sol, at) + value)

        smooth(rhs, mid, emit)
        answer(out_sol if first else corr, tags, (out_own, out_next))


def lift_kernel(parent, sol, in_own, in_next, out_sol, *refs):
    out, (lift, face) = refs[:6], refs[6:]
    sec, blk = position()
    j, k = lane_parts()

    def pack(make, g, _):
        planes = make(g)
        zero = jnp.zeros((8, 128), F32)
        y_low, y_high, z_low, z_high = [zero] * 2, [zero] * 2, [zero] * 4, [zero] * 4
        for m, a in enumerate(planes):
            y_mask, z_mask = j == m, k == m
            for p in range(2):
                y_low[p] = jnp.where(y_mask, roll(a[0][p], 16 * m), y_low[p])
                y_high[p] = jnp.where(y_mask, roll(a[3][p], (16 * m + 16) % 128), y_high[p])
            for r in range(4):
                z_low[r] = jnp.where(z_mask, roll(a[r][0], m), z_low[r])
                z_high[r] = jnp.where(z_mask, roll(a[r][1], (m + 113) % 128), z_high[r])
        for m, a in enumerate(planes):
            put_plane(out_sol, 8 * g + m, a)
        for o in range(2):
            put(face, 128 + (o * 4 + g) * 8, y_low[o])
            put(face, 192 + (o * 4 + g) * 8, y_high[o])
        half = g & 1
        here = (k >> 3) == half
        for q in range(4):
            at = 256 + (q * 2 + (g >> 1)) * 8
            put(face, at, jnp.where(here, roll(z_low[q], 8 * half), rows(face, at)))
            put(face, at + 64, jnp.where(here, roll(z_high[q], 8 * half), rows(face, at + 64)))
        return 0

    @pl.when(sec == 0)
    def _():
        for g, (to_own, to_next, own_slot, next_slot, _) in enumerate(parent_slots(parent, blk)):
            at = pl.ds(g, 32, stride=8)

            @pl.when(to_own)
            def _(at=at, slot=own_slot):
                lift[at, :] = rows(in_own, slot * 32, 32)

            @pl.when(to_next)
            def _(at=at, slot=next_slot):
                lift[at, :] = rows(in_next, slot * 32, 32)

            @pl.when(jnp.logical_not(to_own | to_next))
            def _(at=at):
                lift[at, :] = jnp.zeros((32, 128), F32)

        def lifted(g):
            planes = [plane(sol, 8 * g + m) for m in range(8)]
            for m in range(4):
                for s in range(2):
                    value = rows(lift, (s * 16 + 4 * g + m) * 8)
                    for x in (2 * m, 2 * m + 1):
                        for r in (2 * s, 2 * s + 1):
                            planes[x][r] = [planes[x][r][p] + value for p in range(2)]
            return planes

        lax.fori_loop(0, 4, functools.partial(pack, lifted), 0)

    @pl.when(sec == 1)
    def _():
        lax.fori_loop(0, 4, functools.partial(pack, lambda g: [plane(sol, 8 * g + m) for m in range(8)]), 0)

    put(face, 0, rows(out_sol, 64, 64))
    put(face, 64, rows(out_sol, 32 * 64, 64))
    for axis, parity in enumerate(parities(blk)):
        for color in range(2):
            d = 2 * axis + (parity == color).astype(jnp.int32)
            out[2 * axis + color][...] = rows(face, d * 64, 64)


def residual_kernel(last, parent, neighbor, src, sol, *refs):
    sent, got = refs[:6], refs[6:12]
    if last:
        res, halo, table = refs[12:]
    else:
        res, own, nxt, halo, table, down = refs[12:]
    sec, blk = position()
    j, k = lane_parts()

    for axis, parity in enumerate(parities(blk)):
        for color in range(2):
            odd = (parity == color).astype(jnp.int32)
            put(table, (2 * axis + 1 - odd) * 128, sent[2 * axis + color][...])
            put(table, (2 * axis + odd) * 128 + 64, got[2 * axis + color][...])
    device = sec * N_BLK + blk

    def gather(g, _):
        for d in range(6):
            other = neighbor[g, d]
            local = (other >> 3) == device
            start = d * 128 + jnp.where(local, 0, 64) + (other & 7)
            value = table[pl.ds(start, 8, stride=8), :]
            halo[pl.ds(d * 64 + g, 8, stride=8), :] = jnp.where(other >= 0, value, 0.0)
        return 0

    lax.fori_loop(0, FAM, gather, 0)

    def side(base):
        return [[rows(halo, base + (q * 2 + o) * 8) for o in range(2)] for q in range(4)]

    def residue(x, a, below, above):
        y_at, z_at = x & 7, x & 15
        y_rows = [128 + (o * 4 + (x >> 3)) * 8 for o in range(2)]
        hy = [
            [roll(rows(halo, y_rows[o]), (128 - 16 * y_at) & 127) for o in range(2)],
            [roll(rows(halo, y_rows[o] + 64), 112 - 16 * y_at) for o in range(2)],
        ]
        hz = []
        for q in range(4):
            at = 256 + (q * 2 + (x >> 4)) * 8
            hz.append([roll(rows(halo, at), (128 - z_at) & 127), roll(rows(halo, at + 64), 15 - z_at)])
        m = around(a, below, above, j, k, hy, hz)
        s = plane(src, x)
        return [[s[q][o] - 6.0 * a[q][o] + m[q][o] for o in range(2)] for q in range(4)]

    def store(x, r):
        if last:
            put_given(res, x, to_given(r, j, k))
        else:
            put_plane(res, x, r)

    def group(i, _, low=None, high=None):
        x = GROUP * i
        p = [plane(sol, x + m) for m in range(GROUP)]
        p = [plane(sol, x - 1) if low is None else low] + p + [plane(sol, x + GROUP) if high is None else high]
        r = [residue(x + m, p[m + 1], p[m], p[m + 2]) for m in range(GROUP)]
        for m in range(GROUP):
            store(x + m, r[m])
        if not last:
            for m in range(GROUP // 2):
                put_down(down, (GROUP // 2) * i + m, restrict_pair(r[2 * m], r[2 * m + 1]))
        return 0

    count = 32 // GROUP
    group(0, 0, low=side(0))
    lax.fori_loop(1, count - 1, group, 0)
    group(count - 1, 0, high=side(64))
    if not last:

        @pl.when(sec == 0)
        def _():
            send_down(down, parent, blk, own, nxt, False)


def fine_kernel(res, sol, out_sol, rhs, mid):
    sec, _ = position()

    @pl.when(sec == 1)
    def _():
        def copy(i, _):
            put(out_sol, i * 64, rows(sol, i * 64, 64))
            return 0

        lax.fori_loop(1, 33, copy, 0)

    @pl.when(sec == 0)
    def _():
        def copy(i, _):
            put(rhs, i * 64, rows(res, i * 64, 64))
            return 0

        lax.fori_loop(1, 33, copy, 0)

        def emit(at, value):
            put(out_sol, at, rows(sol, at) + value)

        smooth(rhs, mid, emit)


def unload_kernel(sol, out):
    j, k = lane_parts()

    def convert(i, _):
        planes = [to_given(plane(sol, GROUP * i + m), j, k) for m in range(GROUP)]
        for m in range(GROUP):
            put_given(out, GROUP * i + m, planes[m])
        return 0

    lax.fori_loop(0, 32 // GROUP, convert, 0)


def shape(n, dtype=F32):
    return jax.ShapeDtypeStruct((n, 128), dtype)


def scratch(n):
    return pltpu.VMEM((n, 128), F32)


def call(kernel, name, in_specs, out_shape, scratch_shapes=(), out_specs=None):
    return pl.pallas_call(
        kernel,
        name=name,
        in_specs=in_specs,
        out_shape=out_shape,
        out_specs=out_specs or [VMEM] * len(out_shape),
        scratch_shapes=list(scratch_shapes),
        compiler_params=pltpu.CompilerParams(vmem_limit_bytes=32 << 20),
    )


def local(source, parent, neighbor):
    tiles = source.reshape(FAM, 8, 32, 128).transpose(0, 2, 1, 3).reshape(2048, 128)
    pad, pads = shape(PAD_ROWS), scratch(PAD_ROWS)

    def both(own, nxt):
        return swap(nxt, NEXT_PAIRS), swap(own, OWN_PAIRS)

    own, nxt = call(first_down_kernel, "first_down", [SMEM, VMEM], (shape(136), shape(136)), [scratch(256)])(
        parent, tiles
    )
    got_next, got_own = both(own, nxt)
    src, sol = call(load_kernel, "load", [VMEM], (pad, pad), [pads])(tiles)
    res, tags = src, None
    for iteration in range(2):
        first = iteration == 0
        if first:
            sol, own, nxt, tags = call(
                lambda *refs: coarse_kernel(True, *refs),
                "coarse_0",
                [VMEM] * 4,
                (pad, shape(128), shape(128), jax.ShapeDtypeStruct((8,), jnp.int32)),
                [pads, pads, pltpu.SMEM((2, 8, 128), F32), pltpu.SemaphoreType.DMA((2,))],
                [VMEM, VMEM, VMEM, SMEM],
            )(res, sol, got_own, got_next)
        else:
            sol, own, nxt = call(
                lambda *refs: coarse_kernel(False, *refs),
                "coarse_1",
                [SMEM] + [VMEM] * 4,
                (pad, shape(128), shape(128)),
                [pads, pads, pads],
            )(tags, res, sol, got_own, got_next)
        got_next, got_own = both(own, nxt)
        out = call(
            lift_kernel,
            f"lift_{iteration}",
            [SMEM, VMEM, VMEM, VMEM],
            (pad,) + (shape(64),) * 6,
            [scratch(256), scratch(384)],
        )(parent, sol, got_own, got_next)
        sol, sent = out[0], out[1:]
        got = [swap(s, pairs) for s, pairs in zip(sent, HALO_PAIRS)]
        ins = [SMEM, SMEM] + [VMEM] * 14
        if first:
            res, own, nxt = call(
                lambda *refs: residual_kernel(False, *refs),
                "residual_0",
                ins,
                (pad, shape(128), shape(128)),
                [scratch(384), scratch(768), scratch(256)],
            )(parent, neighbor, src, sol, *sent, *got)
            got_next, got_own = both(own, nxt)
            (sol,) = call(fine_kernel, "fine", [VMEM, VMEM], (pad,), [pads, pads])(res, sol)
        else:
            (solution,) = call(unload_kernel, "unload", [VMEM], (shape(2048),))(sol)
            (residual,) = call(
                lambda *refs: residual_kernel(True, *refs),
                "residual_1",
                ins,
                (shape(2048),),
                [scratch(384), scratch(768)],
            )(parent, neighbor, src, sol, *sent, *got)

    def blocks(x):
        return x.reshape(FAM, 32, 8, 128).transpose(0, 2, 1, 3).reshape(64, 4096)

    return blocks(solution), blocks(residual)


def solution(mesh):
    return jax.shard_map(
        local,
        mesh=mesh,
        in_specs=(P(AX, None), P(AX), P(AX, None)),
        out_specs=(P(AX, None), P(AX, None)),
        check_vma=False,
    )
```

```python
import functools

import jax
import jax.numpy as jnp
from jax import lax
from jax.experimental import pallas as pl
from jax.experimental.pallas import tpu as pltpu
from jax.sharding import PartitionSpec as P

AX = ("sec", "blk")
N_BLK = 64
FAM = 8
WEIGHT = 0.8 / 6.0
PAD_ROWS = 34 * 64
GROUP = 4
F32 = jnp.float32
VMEM = pl.BlockSpec(memory_space=pltpu.VMEM)
SMEM = pl.BlockSpec(memory_space=pltpu.SMEM)


def swap_pairs(unit, color):
    pairs, used = [], set()
    for b in range(N_BLK - unit):
        if (b // unit) % 2 == color:
            for s in (0, N_BLK):
                pairs += [(s + b, s + b + unit), (s + b + unit, s + b)]
            used |= {b, b + unit}
    for b in range(N_BLK):
        if b not in used:
            pairs += [(b, N_BLK + b), (N_BLK + b, b)]
    return pairs


def level_pairs():
    own, down, up = [], [], []
    for b in range(N_BLK):
        c, beyond = N_BLK + b, N_BLK + (b + 1) % N_BLK
        own += [(b, c), (c, b)]
        down += [(b, beyond), (c, b)]
        up += [(beyond, b), (b, c)]
    return own, down, up


UNITS = (16, 4, 1)
ORDER = (4, 5, 2, 3, 0, 1)
HALO_PAIRS = [swap_pairs(unit, color) for unit in UNITS for color in (0, 1)]
OWN_PAIRS, DOWN_PAIRS, UP_PAIRS = level_pairs()


def swap(x, pairs):
    return lax.ppermute(x, AX, pairs)


def position():
    return lax.axis_index("sec"), lax.axis_index("blk")


def parities(blk):
    return [(blk >> 4) & 1, (blk >> 2) & 1, blk & 1]


def lane_parts():
    lane = lax.broadcasted_iota(jnp.int32, (8, 128), 1)
    return lane >> 4, lane & 15


def roll(x, by):
    return pltpu.roll(x, by, 1)


def rows(ref, start, size=8):
    return ref[pl.ds(pl.multiple_of(start, 8), size), :]


def put(ref, start, value):
    ref[pl.ds(pl.multiple_of(start, 8), value.shape[0]), :] = value


def plane(ref, x):
    base = (x + 1) * 64
    return [[rows(ref, base + (q * 2 + oz) * 8) for oz in range(2)] for q in range(4)]


def around(a, below, above, j, k, hy=None, hz=None):
    zero = jnp.zeros((8, 128), F32)
    if hy is None:
        hy = [[zero, zero], [zero, zero]]
    if hz is None:
        hz = [[zero, zero] for _ in range(4)]
    y_low = [jnp.where(j == 0, hy[0][p], roll(a[3][p], 16)) for p in range(2)]
    y_high = [jnp.where(j == 7, hy[1][p], roll(a[0][p], 112)) for p in range(2)]
    total = []
    for r in range(4):
        z_low = jnp.where(k == 0, hz[r][0], roll(a[r][1], 1))
        z_high = jnp.where(k == 15, hz[r][1], roll(a[r][0], 127))
        line = []
        for p in range(2):
            y_sum = (a[r - 1][p] if r else y_low[p]) + (a[r + 1][p] if r < 3 else y_high[p])
            z_sum = a[r][1 - p] + (z_high if p else z_low)
            line.append((y_sum + z_sum) + (below[r][p] + above[r][p]))
        total.append(line)
    return total


def exchange(a, b, bit, partner):
    moved = jnp.take_along_axis(jnp.where(bit, a, b), partner, axis=1)
    return jnp.where(bit, moved, a), jnp.where(bit, b, moved)


def lane_bits(j, k):
    lane = j * 16 + k
    return [((lane & m) != 0, lane ^ m) for m in (1, 16, 32)]


def spread_index(j, k):
    return ((j & 1) * 4 + (j >> 1)) * 16 + 2 * (k & 7) + (k >> 3)


def to_working(v, j, k):
    z_bit, y_bit, y_next = lane_bits(j, k)
    s = [exchange(v[q][0], v[q][1], *z_bit) for q in range(4)]
    index = spread_index(j, k)
    result = [[None, None] for _ in range(4)]
    for p in range(2):
        t = [exchange(s[2 * h][p], s[2 * h + 1][p], *y_bit) for h in range(2)]
        for low in range(2):
            pair = exchange(t[0][low], t[1][low], *y_next)
            for high in range(2):
                result[low + 2 * high][p] = jnp.take_along_axis(pair[high], index, axis=1)
    return result


def to_given(a, j, k):
    z_bit, y_bit, y_next = lane_bits(j, k)
    index = (2 * (j & 3) + (j >> 2)) * 16 + (k >> 1) + 8 * (k & 1)
    s = [[None, None] for _ in range(4)]
    for p in range(2):
        t = [[None, None], [None, None]]
        for low in range(2):
            pair = [jnp.take_along_axis(a[low + 2 * high][p], index, axis=1) for high in range(2)]
            t[0][low], t[1][low] = exchange(pair[0], pair[1], *y_next)
        for h in range(2):
            s[2 * h][p], s[2 * h + 1][p] = exchange(t[h][0], t[h][1], *y_bit)
    return [exchange(s[q][0], s[q][1], *z_bit) for q in range(4)]


def given_rows(x, q, oz):
    octant = (x >> 4) * 4 + (q // 2) * 2 + oz
    return pl.ds(((x & 15) * 2 + q % 2) * 8 + octant, 8, stride=256)


def given_plane(ref, x):
    return [[ref[given_rows(x, q, oz), :] for oz in range(2)] for q in range(4)]


def put_given(ref, x, v):
    for q in range(4):
        for oz in range(2):
            ref[given_rows(x, q, oz), :] = v[q][oz]


def put_plane(ref, x, a):
    for r in range(4):
        for p in range(2):
            put(ref, (x + 1) * 64 + (r * 2 + p) * 8, a[r][p])


def clear_pads(ref):
    for start in (0, 33 * 64):
        ref[start : start + 64, :] = jnp.zeros((64, 128), F32)


def smooth(rhs, mid, emit):
    j, k = lane_parts()
    clear_pads(rhs)
    clear_pads(mid)

    def sweep(src, write):
        def body(i, _):
            x0 = i * GROUP
            p = [plane(src, x0 + m - 1) for m in range(GROUP + 2)]
            result = [around(p[m + 1], p[m], p[m + 2], j, k) for m in range(GROUP)]
            for m in range(GROUP):
                for r in range(4):
                    for c in range(2):
                        write((x0 + m + 1) * 64 + (r * 2 + c) * 8, p[m + 1][r][c], result[m][r][c])
            return 0

        lax.fori_loop(0, 32 // GROUP, body, 0)

    def first(at, a, m):
        put(mid, at, 1.2 * a + WEIGHT * m)

    def second(at, a, m):
        emit(at, WEIGHT * (rows(rhs, at) + 0.2 * a + WEIGHT * m))

    sweep(rhs, first)
    sweep(mid, second)


def put_down(down, i, pair):
    for r in range(2):
        put(down, (r * 16 + i) * 8, pair[r])


def restrict_pair(a, b):
    c = [[a[r][p] + b[r][p] for p in range(2)] for r in range(4)]
    return [0.5 * ((c[2 * r][0] + c[2 * r][1]) + (c[2 * r + 1][0] + c[2 * r + 1][1])) for r in range(2)]


def restrict_given(a, b, j, k):
    z_even, y_even = (k & 1) == 0, (j & 1) == 0
    u = []
    for q in range(4):
        lo, hi = a[q][0] + b[q][0], a[q][1] + b[q][1]
        u.append(jnp.where(z_even, lo + roll(lo, 127), hi + roll(hi, 1)))
    m = []
    for h in range(2):
        m.append(jnp.where(y_even, u[2 * h] + roll(u[2 * h], 112), u[2 * h + 1] + roll(u[2 * h + 1], 16)))
    index = spread_index(j, k)
    return [0.5 * jnp.take_along_axis(n, index, axis=1) for n in exchange(m[0], m[1], *lane_bits(j, k)[2])]


def parent_slots(parent, blk):
    own_count, next_count = jnp.int32(0), jnp.int32(0)
    found = []
    for g in range(FAM):
        value = parent[g]
        chip = (value >> 6) - N_BLK
        to_own = (value >= 0) & (chip == blk)
        to_next = (value >= 0) & (chip == ((blk + 1) & (N_BLK - 1)))
        found.append((to_own, to_next, own_count, next_count, value & 63))
        own_count = own_count + to_own.astype(jnp.int32)
        next_count = next_count + to_next.astype(jnp.int32)
    return found


def send_down(down, parent, blk, own, nxt, tags):
    for buf in (own, nxt):
        if tags:
            buf[128:136, :] = jnp.full((8, 128), -1.0, F32)
    for g, (to_own, to_next, own_slot, next_slot, block) in enumerate(parent_slots(parent, blk)):
        for going, slot, buf in ((to_own, own_slot, own), (to_next, next_slot, nxt)):

            @pl.when(going)
            def _(slot=slot, buf=buf, block=block, g=g):
                put(buf, slot * 32, down[pl.ds(g, 32, stride=8), :])
                if tags:
                    buf[pl.ds(128 + slot, 1), :] = jnp.full((1, 128), block.astype(F32), F32)


def block_place(block, s, half):
    f, o = block >> 3, block & 7
    start = ((o >> 2) * 16 + 8 * half + 1) * 64 + f
    at = [[pl.ds(start + ((2 * t + s) * 2 + p) * 8, 8, stride=64) for p in range(2)] for t in range(2)]
    return at, (o >> 1) & 1, o & 1


def add_incoming(rhs, tags, arrived):
    j, k = lane_parts()
    index = [[(2 * (j & 3) + t) * 16 + 2 * (k & 7) + p for p in range(2)] for t in range(2)]
    for n in range(8):
        buf, slot, tag = arrived[n // 4], n % 4, tags[n]

        used, block = tag >= 0, jnp.maximum(tag, 0)
        places, spread = [], []
        for s in range(2):
            for half in range(2):
                at, oy, oz = block_place(block, s, half)
                here = ((j >> 2) == jnp.where(used, oy, -1)) & ((k >> 3) == oz)
                value = rows(buf, slot * 32 + s * 16 + half * 8)
                for t in range(2):
                    for p in range(2):
                        places.append(at[t][p])
                        spread.append(jnp.where(here, jnp.take_along_axis(value, index[t][p], axis=1), 0.0))
        total = [rhs[at, :] + value for at, value in zip(places, spread)]
        for at, value in zip(places, total):
            rhs[at, :] = value


def answer(correction, tags, out):
    j, k = lane_parts()
    y_odd, z_odd = (j & 1) == 1, (k & 1) == 1
    for n in range(8):
        buf, slot, tag = out[n // 4], n % 4, tags[n]

        block = jnp.maximum(tag, 0)
        found = []
        for s in range(2):
            for half in range(2):
                at, oy, oz = block_place(block, s, half)
                index = (4 * oy + (j >> 1)) * 16 + 8 * oz + (k >> 1)
                v = [[jnp.take_along_axis(correction[at[t][p], :], index, axis=1) for p in range(2)] for t in range(2)]
                v = [jnp.where(z_odd, v[t][1], v[t][0]) for t in range(2)]
                found.append(jnp.where(y_odd, v[1], v[0]))
        for i, value in enumerate(found):
            put(buf, slot * 32 + i * 8, value)


def first_down_kernel(parent, source, nxt, own, down):
    sec, blk = position()
    j, k = lane_parts()

    @pl.when(sec == 0)
    def _():
        def pair(i):
            return restrict_given(given_plane(source, 2 * i), given_plane(source, 2 * i + 1), j, k)

        def pairs(n, _):
            done = [pair(4 * n + m) for m in range(4)]
            for m in range(4):
                put_down(down, 4 * n + m, done[m])
            return 0

        lax.fori_loop(0, 4, pairs, 0)
        send_down(down, parent, blk, own, nxt, True)


def load_kernel(source, src, sol, mid):
    sec, _ = position()

    j, k = lane_parts()

    def convert(i, _):
        planes = [to_working(given_plane(source, GROUP * i + m), j, k) for m in range(GROUP)]
        for m in range(GROUP):
            put_plane(src, GROUP * i + m, planes[m])
        return 0

    lax.fori_loop(0, 32 // GROUP, convert, 0)

    @pl.when(sec == 0)
    def _():
        def emit(at, value):
            put(sol, at, value)

        smooth(src, mid, emit)


def coarse_kernel(first, *refs):
    if first:
        res, in_next, in_own, out_sol, out_next, out_own, tags, rhs, mid, smem, sem = refs
    else:
        tags, res, sol, _, in_next, in_own, out_sol, out_next, out_own, rhs, mid, corr = refs
    sec, _ = position()

    if first:
        for j in range(8):
            tags[j] = jnp.int32(-1)

    @pl.when(sec == 1)
    def _():
        if first:
            copies = [
                pltpu.make_async_copy(buf.at[128:136, :], smem.at[k], sem.at[k])
                for k, buf in enumerate((in_own, in_next))
            ]
            for c in copies:
                c.start()

        def copy(i, _):
            put(rhs, i * 64, rows(res, i * 64, 64))
            return 0

        lax.fori_loop(1, 33, copy, 0)
        if first:
            for k, c in enumerate(copies):
                c.wait()
                for j in range(4):
                    tags[k * 4 + j] = smem[k, j, 0].astype(jnp.int32)
        add_incoming(rhs, tags, (in_own, in_next))

        def emit(at, value):
            if first:
                put(out_sol, at, value)
            else:
                put(corr, at, value)
                put(out_sol, at, rows(sol, at) + value)

        smooth(rhs, mid, emit)
        answer(out_sol if first else corr, tags, (out_own, out_next))


def lift_kernel(parent, sol, coarse_sol, in_next, in_own, out_sol, *refs):
    out, (lift, face) = refs[:6], refs[6:]
    sec, blk = position()
    j, k = lane_parts()

    def pack(make, g, _):
        planes = make(g)
        zero = jnp.zeros((8, 128), F32)
        y_low, y_high, z_low, z_high = [zero] * 2, [zero] * 2, [zero] * 4, [zero] * 4
        for m, a in enumerate(planes):
            y_mask, z_mask = j == m, k == m
            for p in range(2):
                y_low[p] = jnp.where(y_mask, roll(a[0][p], 16 * m), y_low[p])
                y_high[p] = jnp.where(y_mask, roll(a[3][p], (16 * m + 16) % 128), y_high[p])
            for r in range(4):
                z_low[r] = jnp.where(z_mask, roll(a[r][0], m), z_low[r])
                z_high[r] = jnp.where(z_mask, roll(a[r][1], (m + 113) % 128), z_high[r])
        for m, a in enumerate(planes):
            put_plane(out_sol, 8 * g + m, a)
        for o in range(2):
            put(face, 128 + (o * 4 + g) * 8, y_low[o])
            put(face, 192 + (o * 4 + g) * 8, y_high[o])
        half = g & 1
        here = (k >> 3) == half
        for q in range(4):
            at = 256 + (q * 2 + (g >> 1)) * 8
            put(face, at, jnp.where(here, roll(z_low[q], 8 * half), rows(face, at)))
            put(face, at + 64, jnp.where(here, roll(z_high[q], 8 * half), rows(face, at + 64)))
        return 0

    @pl.when(sec == 0)
    def _():
        for g, (to_own, to_next, own_slot, next_slot, _) in enumerate(parent_slots(parent, blk)):
            at = pl.ds(g, 32, stride=8)

            @pl.when(to_own)
            def _(at=at, slot=own_slot):
                lift[at, :] = rows(in_own, slot * 32, 32)

            @pl.when(to_next)
            def _(at=at, slot=next_slot):
                lift[at, :] = rows(in_next, slot * 32, 32)

            @pl.when(jnp.logical_not(to_own | to_next))
            def _(at=at):
                lift[at, :] = jnp.zeros((32, 128), F32)

        def lifted(g):
            planes = [plane(sol, 8 * g + m) for m in range(8)]
            for m in range(4):
                for s in range(2):
                    value = rows(lift, (s * 16 + 4 * g + m) * 8)
                    for x in (2 * m, 2 * m + 1):
                        for r in (2 * s, 2 * s + 1):
                            planes[x][r] = [planes[x][r][p] + value for p in range(2)]
            return planes

        lax.fori_loop(0, 4, functools.partial(pack, lifted), 0)

    @pl.when(sec == 1)
    def _():
        lax.fori_loop(0, 4, functools.partial(pack, lambda g: [plane(coarse_sol, 8 * g + m) for m in range(8)]), 0)

    put(face, 0, rows(out_sol, 64, 64))
    put(face, 64, rows(out_sol, 32 * 64, 64))
    for axis, parity in enumerate(parities(blk)):
        for color in range(2):
            d = 2 * axis + (parity == color).astype(jnp.int32)
            out[ORDER.index(2 * axis + color)][...] = rows(face, d * 64, 64)


def residual_kernel(level, parent, neighbor, src, sol, *refs):
    sent, got = ([refs[first + ORDER.index(n)] for n in range(6)] for first in (0, 6))
    last, fine = level is None, level == 0
    if fine:
        res, nxt, own, halo, table, down = refs[12:]
    else:
        res, halo, table = refs[12:]
    sec, blk = position()

    def whole():
        j, k = lane_parts()

        for axis, parity in enumerate(parities(blk)):
            for color in range(2):
                odd = (parity == color).astype(jnp.int32)
                put(table, (2 * axis + 1 - odd) * 128, sent[2 * axis + color][...])
                put(table, (2 * axis + odd) * 128 + 64, got[2 * axis + color][...])
        device = sec * N_BLK + blk

        def gather(g, _):
            for d in range(6):
                other = neighbor[g, d]
                local = (other >> 3) == device
                start = d * 128 + jnp.where(local, 0, 64) + (other & 7)
                value = table[pl.ds(start, 8, stride=8), :]
                halo[pl.ds(d * 64 + g, 8, stride=8), :] = jnp.where(other >= 0, value, 0.0)
            return 0

        lax.fori_loop(0, FAM, gather, 0)

        def side(base):
            return [[rows(halo, base + (q * 2 + o) * 8) for o in range(2)] for q in range(4)]

        def residue(x, a, below, above):
            y_at, z_at = x & 7, x & 15
            y_rows = [128 + (o * 4 + (x >> 3)) * 8 for o in range(2)]
            hy = [
                [roll(rows(halo, y_rows[o]), (128 - 16 * y_at) & 127) for o in range(2)],
                [roll(rows(halo, y_rows[o] + 64), 112 - 16 * y_at) for o in range(2)],
            ]
            hz = []
            for q in range(4):
                at = 256 + (q * 2 + (x >> 4)) * 8
                hz.append([roll(rows(halo, at), (128 - z_at) & 127), roll(rows(halo, at + 64), 15 - z_at)])
            m = around(a, below, above, j, k, hy, hz)
            s = plane(src, x)
            return [[s[q][o] - 6.0 * a[q][o] + m[q][o] for o in range(2)] for q in range(4)]

        def store(x, r):
            if last:
                put_given(res, x, to_given(r, j, k))
            else:
                put_plane(res, x, r)

        def group(i, _, low=None, high=None):
            x = GROUP * i
            p = [plane(sol, x + m) for m in range(GROUP)]
            p = [plane(sol, x - 1) if low is None else low] + p + [plane(sol, x + GROUP) if high is None else high]
            r = [residue(x + m, p[m + 1], p[m], p[m + 2]) for m in range(GROUP)]
            for m in range(GROUP):
                store(x + m, r[m])
            if fine:
                for m in range(GROUP // 2):
                    put_down(down, (GROUP // 2) * i + m, restrict_pair(r[2 * m], r[2 * m + 1]))
            return 0

        count = 32 // GROUP
        group(0, 0, low=side(0))
        lax.fori_loop(1, count - 1, group, 0)
        group(count - 1, 0, high=side(64))
        if fine:
            send_down(down, parent, blk, own, nxt, False)

    if last:
        whole()
    else:
        pl.when(sec == level)(whole)


def fine_kernel(res, sol, out_sol, rhs, mid):
    sec, _ = position()

    @pl.when(sec == 0)
    def _():
        def copy(i, _):
            put(rhs, i * 64, rows(res, i * 64, 64))
            return 0

        lax.fori_loop(1, 33, copy, 0)

        def emit(at, value):
            put(out_sol, at, rows(sol, at) + value)

        smooth(rhs, mid, emit)


def unload_kernel(sol, out):
    j, k = lane_parts()

    def convert(i, _):
        planes = [to_given(plane(sol, GROUP * i + m), j, k) for m in range(GROUP)]
        for m in range(GROUP):
            put_given(out, GROUP * i + m, planes[m])
        return 0

    lax.fori_loop(0, 32 // GROUP, convert, 0)


def shape(n, dtype=F32):
    return jax.ShapeDtypeStruct((n, 128), dtype)


def scratch(n):
    return pltpu.VMEM((n, 128), F32)


def call(kernel, name, in_specs, out_shape, scratch_shapes=(), out_specs=None):
    return pl.pallas_call(
        kernel,
        name=name,
        in_specs=in_specs,
        out_shape=out_shape,
        out_specs=out_specs or [VMEM] * len(out_shape),
        scratch_shapes=list(scratch_shapes),
        compiler_params=pltpu.CompilerParams(vmem_limit_bytes=32 << 20),
    )


def local(source, parent, neighbor):
    tiles = source.reshape(FAM, 8, 32, 128).transpose(0, 2, 1, 3).reshape(2048, 128)
    pad, pads = shape(PAD_ROWS), scratch(PAD_ROWS)

    def both(nxt, own, pairs):
        return swap(nxt, pairs), swap(own, OWN_PAIRS)

    nxt, own = call(first_down_kernel, "first_down", [SMEM, VMEM], (shape(136), shape(136)), [scratch(256)])(
        parent, tiles
    )
    got_next, got_own = both(nxt, own, DOWN_PAIRS)
    src, fine_sol = call(load_kernel, "load", [VMEM], (pad, pad), [pads])(tiles)
    coarse_sol, nxt, own, tags = call(
        functools.partial(coarse_kernel, True),
        "coarse_0",
        [VMEM] * 3,
        (pad, shape(128), shape(128), jax.ShapeDtypeStruct((8,), jnp.int32)),
        [pads, pads, pltpu.SMEM((2, 8, 128), F32), pltpu.SemaphoreType.DMA((2,))],
        [VMEM, VMEM, VMEM, SMEM],
    )(src, got_next, got_own)

    def lift_and_share(n, nxt, own):
        got_next, got_own = both(nxt, own, UP_PAIRS)
        out = call(
            lift_kernel,
            f"lift_{n}",
            [SMEM] + [VMEM] * 4,
            (pad,) + (shape(64),) * 6,
            [scratch(256), scratch(384)],
        )(parent, fine_sol, coarse_sol, got_next, got_own)
        sol, sent = out[0], out[1:]
        return sol, [*sent, *(swap(face, HALO_PAIRS[n]) for face, n in zip(sent, ORDER))]

    def residue_of(level, name, sol, faces, out_shape, more=()):
        return call(
            functools.partial(residual_kernel, level),
            name,
            [SMEM, SMEM] + [VMEM] * 14,
            out_shape,
            [scratch(384), scratch(768), *more],
        )(parent, neighbor, src, sol, *faces)

    sol, faces = lift_and_share(0, nxt, own)
    res, nxt, own = residue_of(0, "residue_fine", sol, faces, (pad, shape(128), shape(128)), [scratch(256)])
    got_next, got_own = both(nxt, own, DOWN_PAIRS)
    (coarse_res,) = residue_of(1, "residue_coarse", sol, faces, (pad,))
    (fine_sol,) = call(fine_kernel, "fine", [VMEM, VMEM], (pad,), [pads, pads])(res, sol)
    coarse_sol, nxt, own = call(
        functools.partial(coarse_kernel, False),
        "coarse_1",
        [SMEM] + [VMEM] * 5,
        (pad, shape(128), shape(128)),
        [pads, pads, pads],
    )(tags, coarse_res, sol, fine_sol, got_next, got_own)
    sol, faces = lift_and_share(1, nxt, own)
    (solution,) = call(unload_kernel, "unload", [VMEM], (shape(2048),))(sol)
    (residual,) = residue_of(None, "residual", sol, faces, (shape(2048),))

    def blocks(x):
        return x.reshape(FAM, 32, 8, 128).transpose(0, 2, 1, 3).reshape(64, 4096)

    return blocks(solution), blocks(residual)


def solution(mesh):
    return jax.shard_map(
        local,
        mesh=mesh,
        in_specs=(P(AX, None), P(AX), P(AX, None)),
        out_specs=(P(AX, None), P(AX, None)),
        check_vma=False,
    )
```

```python
import functools

import jax
import jax.numpy as jnp
from jax import lax
from jax.experimental import pallas as pl
from jax.experimental.pallas import tpu as pltpu
from jax.sharding import PartitionSpec as P

AX = ("sec", "blk")
N_BLK = 64
FAM = 8
WEIGHT = 0.8 / 6.0
PAD_ROWS = 34 * 64
SWEEP = 16
RESIDUE = 8
CONVERT = 8
F32 = jnp.float32
VMEM = pl.BlockSpec(memory_space=pltpu.VMEM)
SMEM = pl.BlockSpec(memory_space=pltpu.SMEM)
HBM = pl.BlockSpec(memory_space=pltpu.HBM)


def swap_pairs(unit, color):
    pairs, used = [], set()
    for b in range(N_BLK - unit):
        if (b // unit) % 2 == color:
            for s in (0, N_BLK):
                pairs += [(s + b, s + b + unit), (s + b + unit, s + b)]
            used |= {b, b + unit}
    for b in range(N_BLK):
        if b not in used:
            pairs += [(b, N_BLK + b), (N_BLK + b, b)]
    return pairs


def level_pairs():
    own, down, up = [], [], []
    for b in range(N_BLK):
        c, beyond = N_BLK + b, N_BLK + (b + 1) % N_BLK
        own += [(b, c), (c, b)]
        down += [(b, beyond), (c, b)]
        up += [(beyond, b), (b, c)]
    return own, down, up


UNITS = (16, 4, 1)
ORDER = (4, 5, 2, 3, 0, 1)
HALO_PAIRS = [swap_pairs(unit, color) for unit in UNITS for color in (0, 1)]
OWN_PAIRS, DOWN_PAIRS, UP_PAIRS = level_pairs()


def swap(x, pairs):
    return lax.ppermute(x, AX, pairs)


def position():
    return lax.axis_index("sec"), lax.axis_index("blk")


def parities(blk):
    return [(blk >> 4) & 1, (blk >> 2) & 1, blk & 1]


def lane_parts():
    lane = lax.broadcasted_iota(jnp.int32, (8, 128), 1)
    return lane >> 4, lane & 15


def roll(x, by):
    return pltpu.roll(x, by, 1)


def rows(ref, start, size=8):
    return ref[pl.ds(pl.multiple_of(start, 8), size), :]


def put(ref, start, value):
    ref[pl.ds(pl.multiple_of(start, 8), value.shape[0]), :] = value


def plane(ref, x):
    base = (x + 1) * 64
    return [[rows(ref, base + (q * 2 + oz) * 8) for oz in range(2)] for q in range(4)]


def around(a, below, above, j, k, hy=None, hz=None):
    zero = jnp.zeros((8, 128), F32)
    if hy is None:
        hy = [[zero, zero], [zero, zero]]
    if hz is None:
        hz = [[zero, zero] for _ in range(4)]
    y_low = [jnp.where(j == 0, hy[0][p], roll(a[3][p], 16)) for p in range(2)]
    y_high = [jnp.where(j == 7, hy[1][p], roll(a[0][p], 112)) for p in range(2)]
    total = []
    for r in range(4):
        z_low = jnp.where(k == 0, hz[r][0], roll(a[r][1], 1))
        z_high = jnp.where(k == 15, hz[r][1], roll(a[r][0], 127))
        line = []
        for p in range(2):
            y_sum = (a[r - 1][p] if r else y_low[p]) + (a[r + 1][p] if r < 3 else y_high[p])
            z_sum = a[r][1 - p] + (z_high if p else z_low)
            line.append((y_sum + z_sum) + (below[r][p] + above[r][p]))
        total.append(line)
    return total


def exchange(a, b, bit, partner):
    moved = jnp.take_along_axis(jnp.where(bit, a, b), partner, axis=1)
    return jnp.where(bit, moved, a), jnp.where(bit, b, moved)


def lane_bits(j, k):
    lane = j * 16 + k
    return [((lane & m) != 0, lane ^ m) for m in (1, 16, 32)]


def spread_index(j, k):
    return ((j & 1) * 4 + (j >> 1)) * 16 + 2 * (k & 7) + (k >> 3)


def to_working(v, j, k):
    z_bit, y_bit, y_next = lane_bits(j, k)
    s = [exchange(v[q][0], v[q][1], *z_bit) for q in range(4)]
    index = spread_index(j, k)
    result = [[None, None] for _ in range(4)]
    for p in range(2):
        t = [exchange(s[2 * h][p], s[2 * h + 1][p], *y_bit) for h in range(2)]
        for low in range(2):
            pair = exchange(t[0][low], t[1][low], *y_next)
            for high in range(2):
                result[low + 2 * high][p] = jnp.take_along_axis(pair[high], index, axis=1)
    return result


def to_given(a, j, k):
    z_bit, y_bit, y_next = lane_bits(j, k)
    index = (2 * (j & 3) + (j >> 2)) * 16 + (k >> 1) + 8 * (k & 1)
    s = [[None, None] for _ in range(4)]
    for p in range(2):
        t = [[None, None], [None, None]]
        for low in range(2):
            pair = [jnp.take_along_axis(a[low + 2 * high][p], index, axis=1) for high in range(2)]
            t[0][low], t[1][low] = exchange(pair[0], pair[1], *y_next)
        for h in range(2):
            s[2 * h][p], s[2 * h + 1][p] = exchange(t[h][0], t[h][1], *y_bit)
    return [exchange(s[q][0], s[q][1], *z_bit) for q in range(4)]


def given_rows(x, q, oz):
    octant = (x >> 4) * 4 + (q // 2) * 2 + oz
    return pl.ds(((x & 15) * 2 + q % 2) * 8 + octant, 8, stride=256)


def given_plane(ref, x):
    return [[ref[given_rows(x, q, oz), :] for oz in range(2)] for q in range(4)]


def put_given(ref, x, v):
    for q in range(4):
        for oz in range(2):
            ref[given_rows(x, q, oz), :] = v[q][oz]


def half_copies(source, target, sems, half):
    parts = [pl.ds(f * 256 + half * 128, 128) for f in range(FAM)]
    return [pltpu.make_async_copy(source.at[at], target.at[at], sems.at[half, f]) for f, at in enumerate(parts)]


def put_plane(ref, x, a):
    for r in range(4):
        for p in range(2):
            put(ref, (x + 1) * 64 + (r * 2 + p) * 8, a[r][p])


def clear_pads(ref):
    for start in (0, 33 * 64):
        ref[start : start + 64, :] = jnp.zeros((64, 128), F32)


def smooth(rhs, mid, emit):
    j, k = lane_parts()
    clear_pads(rhs)
    clear_pads(mid)

    def sweep(src, write):
        def body(i, _):
            x0 = i * SWEEP
            p = [plane(src, x0 + m - 1) for m in range(SWEEP + 2)]
            result = [around(p[m + 1], p[m], p[m + 2], j, k) for m in range(SWEEP)]
            for m in range(SWEEP):
                for r in range(4):
                    for c in range(2):
                        write((x0 + m + 1) * 64 + (r * 2 + c) * 8, p[m + 1][r][c], result[m][r][c])
            return 0

        lax.fori_loop(0, 32 // SWEEP, body, 0)

    def first(at, a, m):
        put(mid, at, 1.2 * a + WEIGHT * m)

    def second(at, a, m):
        emit(at, WEIGHT * (rows(rhs, at) + 0.2 * a + WEIGHT * m))

    sweep(rhs, first)
    sweep(mid, second)


def put_down(down, i, pair):
    for r in range(2):
        put(down, (r * 16 + i) * 8, pair[r])


def restrict_pair(a, b):
    c = [[a[r][p] + b[r][p] for p in range(2)] for r in range(4)]
    return [0.5 * ((c[2 * r][0] + c[2 * r][1]) + (c[2 * r + 1][0] + c[2 * r + 1][1])) for r in range(2)]


def restrict_given(a, b, j, k):
    z_even, y_even = (k & 1) == 0, (j & 1) == 0
    u = []
    for q in range(4):
        lo, hi = a[q][0] + b[q][0], a[q][1] + b[q][1]
        u.append(jnp.where(z_even, lo + roll(lo, 127), hi + roll(hi, 1)))
    m = []
    for h in range(2):
        m.append(jnp.where(y_even, u[2 * h] + roll(u[2 * h], 112), u[2 * h + 1] + roll(u[2 * h + 1], 16)))
    index = spread_index(j, k)
    return [0.5 * jnp.take_along_axis(n, index, axis=1) for n in exchange(m[0], m[1], *lane_bits(j, k)[2])]


def parent_slots(parent, blk):
    own_count, next_count = jnp.int32(0), jnp.int32(0)
    found = []
    for g in range(FAM):
        value = parent[g]
        chip = (value >> 6) - N_BLK
        to_own = (value >= 0) & (chip == blk)
        to_next = (value >= 0) & (chip == ((blk + 1) & (N_BLK - 1)))
        found.append((to_own, to_next, own_count, next_count, value & 63))
        own_count = own_count + to_own.astype(jnp.int32)
        next_count = next_count + to_next.astype(jnp.int32)
    return found


def send_down(down, parent, blk, own, nxt, tags):
    for buf in (own, nxt):
        if tags:
            buf[128:136, :] = jnp.full((8, 128), -1.0, F32)
    for g, (to_own, to_next, own_slot, next_slot, block) in enumerate(parent_slots(parent, blk)):
        for going, slot, buf in ((to_own, own_slot, own), (to_next, next_slot, nxt)):

            @pl.when(going)
            def _(slot=slot, buf=buf, block=block, g=g):
                put(buf, slot * 32, down[pl.ds(g, 32, stride=8), :])
                if tags:
                    buf[pl.ds(128 + slot, 1), :] = jnp.full((1, 128), block.astype(F32), F32)


def block_place(block, s, half):
    f, o = block >> 3, block & 7
    start = ((o >> 2) * 16 + 8 * half + 1) * 64 + f
    at = [[pl.ds(start + ((2 * t + s) * 2 + p) * 8, 8, stride=64) for p in range(2)] for t in range(2)]
    return at, (o >> 1) & 1, o & 1


def add_incoming(rhs, tags, arrived):
    j, k = lane_parts()
    index = [[(2 * (j & 3) + t) * 16 + 2 * (k & 7) + p for p in range(2)] for t in range(2)]
    for n in range(8):
        buf, slot, tag = arrived[n // 4], n % 4, tags[n]

        used, block = tag >= 0, jnp.maximum(tag, 0)
        places, spread = [], []
        for s in range(2):
            for half in range(2):
                at, oy, oz = block_place(block, s, half)
                here = ((j >> 2) == jnp.where(used, oy, -1)) & ((k >> 3) == oz)
                value = rows(buf, slot * 32 + s * 16 + half * 8)
                for t in range(2):
                    for p in range(2):
                        places.append(at[t][p])
                        spread.append(jnp.where(here, jnp.take_along_axis(value, index[t][p], axis=1), 0.0))
        total = [rhs[at, :] + value for at, value in zip(places, spread)]
        for at, value in zip(places, total):
            rhs[at, :] = value


def answer(correction, tags, out):
    j, k = lane_parts()
    y_odd, z_odd = (j & 1) == 1, (k & 1) == 1
    for n in range(8):
        buf, slot, tag = out[n // 4], n % 4, tags[n]

        block = jnp.maximum(tag, 0)
        found = []
        for s in range(2):
            for half in range(2):
                at, oy, oz = block_place(block, s, half)
                index = (4 * oy + (j >> 1)) * 16 + 8 * oz + (k >> 1)
                v = [[jnp.take_along_axis(correction[at[t][p], :], index, axis=1) for p in range(2)] for t in range(2)]
                v = [jnp.where(z_odd, v[t][1], v[t][0]) for t in range(2)]
                found.append(jnp.where(y_odd, v[1], v[0]))
        for i, value in enumerate(found):
            put(buf, slot * 32 + i * 8, value)


def unload_half(source, given, out, sems, half):
    j, k = lane_parts()

    def convert(n, _):
        first = 16 * n + 8 * half
        planes = [to_given(plane(source, first + m), j, k) for m in range(8)]
        for m in range(8):
            put_given(given, first + m, planes[m])
        return 0

    lax.fori_loop(0, 2, convert, 0)
    for copy in half_copies(given, out, sems, half):
        copy.start()


def finish_unload(given, out, sems):
    for half in range(2):
        for copy in half_copies(given, out, sems, half):
            copy.wait()


def first_down_kernel(parent, tiles, nxt, own, down, source, places, sems, place_sem):
    sec, blk = position()
    j, k = lane_parts()

    @pl.when(sec == 0)
    def _():
        halves = [half_copies(tiles, source, sems, half) for half in range(2)]
        place = pltpu.make_async_copy(parent, places, place_sem)
        for copy in (*halves[0], *halves[1], place):
            copy.start()

        def pair(i):
            return restrict_given(given_plane(source, 2 * i), given_plane(source, 2 * i + 1), j, k)

        for half in range(2):
            for copy in halves[half]:
                copy.wait()

            def pairs(n, _):
                first = 8 * n + 4 * half
                done = [pair(first + m) for m in range(4)]
                for m in range(4):
                    put_down(down, first + m, done[m])
                return 0

            lax.fori_loop(0, 2, pairs, 0)
        place.wait()
        send_down(down, places, blk, own, nxt, True)


def load_kernel(source, src, sol, mid):
    sec, _ = position()

    j, k = lane_parts()

    def convert(i, _):
        planes = [to_working(given_plane(source, CONVERT * i + m), j, k) for m in range(CONVERT)]
        for m in range(CONVERT):
            put_plane(src, CONVERT * i + m, planes[m])
        return 0

    lax.fori_loop(0, 32 // CONVERT, convert, 0)

    @pl.when(sec == 0)
    def _():
        def emit(at, value):
            put(sol, at, value)

        smooth(src, mid, emit)


def coarse_kernel(first, *refs):
    if first:
        res, in_next, in_own, out_sol, out_next, out_own, tags, rhs, mid, smem, sem = refs
    else:
        tags, res, sol, _, in_next, in_own, out_sol, out_next, out_own, rhs, mid, corr = refs
    sec, _ = position()

    if first:
        for j in range(8):
            tags[j] = jnp.int32(-1)

    @pl.when(sec == 1)
    def _():
        if first:
            copies = [
                pltpu.make_async_copy(buf.at[128:136, :], smem.at[k], sem.at[k])
                for k, buf in enumerate((in_own, in_next))
            ]
            for c in copies:
                c.start()

        def copy(i, _):
            put(rhs, i * 64, rows(res, i * 64, 64))
            return 0

        lax.fori_loop(1, 33, copy, 0)
        if first:
            for k, c in enumerate(copies):
                c.wait()
                for j in range(4):
                    tags[k * 4 + j] = smem[k, j, 0].astype(jnp.int32)
        add_incoming(rhs, tags, (in_own, in_next))

        def emit(at, value):
            if first:
                put(out_sol, at, value)
            else:
                put(corr, at, value)
                put(out_sol, at, rows(sol, at) + value)

        smooth(rhs, mid, emit)
        answer(out_sol if first else corr, tags, (out_own, out_next))


def lift_kernel(parent, sol, coarse_sol, in_next, in_own, out_sol, *refs):
    out, (lift, face) = refs[:6], refs[6:]
    sec, blk = position()
    j, k = lane_parts()

    def pack(make, g, _):
        planes = make(g)
        zero = jnp.zeros((8, 128), F32)
        y_low, y_high, z_low, z_high = [zero] * 2, [zero] * 2, [zero] * 4, [zero] * 4
        for m, a in enumerate(planes):
            y_mask, z_mask = j == m, k == m
            for p in range(2):
                y_low[p] = jnp.where(y_mask, roll(a[0][p], 16 * m), y_low[p])
                y_high[p] = jnp.where(y_mask, roll(a[3][p], (16 * m + 16) % 128), y_high[p])
            for r in range(4):
                z_low[r] = jnp.where(z_mask, roll(a[r][0], m), z_low[r])
                z_high[r] = jnp.where(z_mask, roll(a[r][1], (m + 113) % 128), z_high[r])
        for m, a in enumerate(planes):
            put_plane(out_sol, 8 * g + m, a)
        for o in range(2):
            put(face, 128 + (o * 4 + g) * 8, y_low[o])
            put(face, 192 + (o * 4 + g) * 8, y_high[o])
        half = g & 1
        here = (k >> 3) == half
        for q in range(4):
            at = 256 + (q * 2 + (g >> 1)) * 8
            put(face, at, jnp.where(here, roll(z_low[q], 8 * half), rows(face, at)))
            put(face, at + 64, jnp.where(here, roll(z_high[q], 8 * half), rows(face, at + 64)))
        return 0

    @pl.when(sec == 0)
    def _():
        for g, (to_own, to_next, own_slot, next_slot, _) in enumerate(parent_slots(parent, blk)):
            at = pl.ds(g, 32, stride=8)

            @pl.when(to_own)
            def _(at=at, slot=own_slot):
                lift[at, :] = rows(in_own, slot * 32, 32)

            @pl.when(to_next)
            def _(at=at, slot=next_slot):
                lift[at, :] = rows(in_next, slot * 32, 32)

            @pl.when(jnp.logical_not(to_own | to_next))
            def _(at=at):
                lift[at, :] = jnp.zeros((32, 128), F32)

        def lifted(g):
            planes = [plane(sol, 8 * g + m) for m in range(8)]
            for m in range(4):
                for s in range(2):
                    value = rows(lift, (s * 16 + 4 * g + m) * 8)
                    for x in (2 * m, 2 * m + 1):
                        for r in (2 * s, 2 * s + 1):
                            planes[x][r] = [planes[x][r][p] + value for p in range(2)]
            return planes

        lax.fori_loop(0, 4, functools.partial(pack, lifted), 0)

    @pl.when(sec == 1)
    def _():
        lax.fori_loop(0, 4, functools.partial(pack, lambda g: [plane(coarse_sol, 8 * g + m) for m in range(8)]), 0)

    put(face, 0, rows(out_sol, 64, 64))
    put(face, 64, rows(out_sol, 32 * 64, 64))
    for axis, parity in enumerate(parities(blk)):
        for color in range(2):
            d = 2 * axis + (parity == color).astype(jnp.int32)
            out[ORDER.index(2 * axis + color)][...] = rows(face, d * 64, 64)


def residual_kernel(level, parent, neighbor, src, sol, *refs):
    sent, got = ([refs[first + ORDER.index(n)] for n in range(6)] for first in (0, 6))
    last, fine = level is None, level == 0
    if fine:
        res, nxt, own, halo, table, down = refs[12:]
    elif last:
        out, halo, table, res, given, sems = refs[12:]
    else:
        res, halo, table = refs[12:]
    sec, blk = position()

    def whole():
        j, k = lane_parts()

        for axis, parity in enumerate(parities(blk)):
            for color in range(2):
                odd = (parity == color).astype(jnp.int32)
                put(table, (2 * axis + 1 - odd) * 128, sent[2 * axis + color][...])
                put(table, (2 * axis + odd) * 128 + 64, got[2 * axis + color][...])
        device = sec * N_BLK + blk

        def gather(g, _):
            for d in range(6):
                other = neighbor[g, d]
                local = (other >> 3) == device
                start = d * 128 + jnp.where(local, 0, 64) + (other & 7)
                value = table[pl.ds(start, 8, stride=8), :]
                halo[pl.ds(d * 64 + g, 8, stride=8), :] = jnp.where(other >= 0, value, 0.0)
            return 0

        lax.fori_loop(0, FAM, gather, 0)

        def side(base):
            return [[rows(halo, base + (q * 2 + o) * 8) for o in range(2)] for q in range(4)]

        def residue(x, a, below, above):
            y_at, z_at = x & 7, x & 15
            y_rows = [128 + (o * 4 + (x >> 3)) * 8 for o in range(2)]
            hy = [
                [roll(rows(halo, y_rows[o]), (128 - 16 * y_at) & 127) for o in range(2)],
                [roll(rows(halo, y_rows[o] + 64), 112 - 16 * y_at) for o in range(2)],
            ]
            hz = []
            for q in range(4):
                at = 256 + (q * 2 + (x >> 4)) * 8
                hz.append([roll(rows(halo, at), (128 - z_at) & 127), roll(rows(halo, at + 64), 15 - z_at)])
            m = around(a, below, above, j, k, hy, hz)
            s = plane(src, x)
            return [[s[q][o] - 6.0 * a[q][o] + m[q][o] for o in range(2)] for q in range(4)]

        def group(x):
            p = [side(0) if x == 0 else plane(sol, x - 1)]
            p += [plane(sol, x + m) for m in range(RESIDUE)]
            p.append(side(64) if x + RESIDUE == 32 else plane(sol, x + RESIDUE))
            r = [residue(x + m, p[m + 1], p[m], p[m + 2]) for m in range(RESIDUE)]
            for m in range(RESIDUE):
                put_plane(res, x + m, r[m])
            if fine:
                for m in range(0, RESIDUE, 2):
                    put_down(down, (x + m) // 2, restrict_pair(r[m], r[m + 1]))

        for half in range(2):
            for x in range(8 * half, 32, 16):
                for first in range(x, x + 8, RESIDUE):
                    group(first)
            if last:
                unload_half(res, given, out, sems, half)
        if last:
            finish_unload(given, out, sems)
        if fine:
            send_down(down, parent, blk, own, nxt, False)

    if last:
        whole()
    else:
        pl.when(sec == level)(whole)


def fine_kernel(res, sol, out_sol, rhs, mid):
    sec, _ = position()

    @pl.when(sec == 0)
    def _():
        def copy(i, _):
            put(rhs, i * 64, rows(res, i * 64, 64))
            return 0

        lax.fori_loop(1, 33, copy, 0)

        def emit(at, value):
            put(out_sol, at, rows(sol, at) + value)

        smooth(rhs, mid, emit)


def unload_kernel(sol, out, given, sems):
    for half in range(2):
        unload_half(sol, given, out, sems, half)
    finish_unload(given, out, sems)


def shape(n, dtype=F32):
    return jax.ShapeDtypeStruct((n, 128), dtype)


def scratch(n):
    return pltpu.VMEM((n, 128), F32)


def call(kernel, name, in_specs, out_shape, scratch_shapes=(), out_specs=None):
    return pl.pallas_call(
        kernel,
        name=name,
        in_specs=in_specs,
        out_shape=out_shape,
        out_specs=out_specs or [VMEM] * len(out_shape),
        scratch_shapes=list(scratch_shapes),
        compiler_params=pltpu.CompilerParams(vmem_limit_bytes=32 << 20),
    )


def local(source, parent, neighbor):
    tiles = source.reshape(FAM, 8, 32, 128).transpose(0, 2, 1, 3).reshape(2048, 128)
    here = pltpu.with_memory_space_constraint(tiles, pltpu.HBM)
    place = pltpu.with_memory_space_constraint(parent, pltpu.HBM)
    pad, pads = shape(PAD_ROWS), scratch(PAD_ROWS)

    def both(nxt, own, pairs):
        return swap(nxt, pairs), swap(own, OWN_PAIRS)

    nxt, own = call(
        first_down_kernel,
        "first_down",
        [HBM, HBM],
        (shape(136), shape(136)),
        [
            scratch(256),
            scratch(2048),
            pltpu.SMEM((FAM,), jnp.int32),
            pltpu.SemaphoreType.DMA((2, FAM)),
            pltpu.SemaphoreType.DMA,
        ],
    )(place, here)
    got_next, got_own = both(nxt, own, DOWN_PAIRS)
    src, fine_sol = call(load_kernel, "load", [VMEM], (pad, pad), [pads])(tiles)
    coarse_sol, nxt, own, tags = call(
        functools.partial(coarse_kernel, True),
        "coarse_0",
        [VMEM] * 3,
        (pad, shape(128), shape(128), jax.ShapeDtypeStruct((8,), jnp.int32)),
        [pads, pads, pltpu.SMEM((2, 8, 128), F32), pltpu.SemaphoreType.DMA((2,))],
        [VMEM, VMEM, VMEM, SMEM],
    )(src, got_next, got_own)

    def lift_and_share(n, nxt, own):
        got_next, got_own = both(nxt, own, UP_PAIRS)
        out = call(
            lift_kernel,
            f"lift_{n}",
            [SMEM] + [VMEM] * 4,
            (pad,) + (shape(64),) * 6,
            [scratch(256), scratch(384)],
        )(parent, fine_sol, coarse_sol, got_next, got_own)
        sol, sent = out[0], out[1:]
        return sol, [*sent, *(swap(face, HALO_PAIRS[n]) for face, n in zip(sent, ORDER))]

    def residue_of(level, name, sol, faces, out_shape, more=(), out_specs=None):
        return call(
            functools.partial(residual_kernel, level),
            name,
            [SMEM, SMEM] + [VMEM] * 14,
            out_shape,
            [scratch(384), scratch(768), *more],
            out_specs,
        )(parent, neighbor, src, sol, *faces)

    sol, faces = lift_and_share(0, nxt, own)
    res, nxt, own = residue_of(0, "residue_fine", sol, faces, (pad, shape(128), shape(128)), [scratch(256)])
    got_next, got_own = both(nxt, own, DOWN_PAIRS)
    (coarse_res,) = residue_of(1, "residue_coarse", sol, faces, (pad,))
    (fine_sol,) = call(fine_kernel, "fine", [VMEM, VMEM], (pad,), [pads, pads])(res, sol)
    coarse_sol, nxt, own = call(
        functools.partial(coarse_kernel, False),
        "coarse_1",
        [SMEM] + [VMEM] * 5,
        (pad, shape(128), shape(128)),
        [pads, pads, pads],
    )(tags, coarse_res, sol, fine_sol, got_next, got_own)
    sol, faces = lift_and_share(1, nxt, own)
    leave = [scratch(2048), pltpu.SemaphoreType.DMA((2, FAM))]
    (solution,) = call(unload_kernel, "unload", [VMEM], (shape(2048),), leave, [HBM])(sol)
    (residual,) = residue_of(None, "residual", sol, faces, (shape(2048),), [pads, *leave], [HBM])

    def blocks(x):
        return x.reshape(FAM, 32, 8, 128).transpose(0, 2, 1, 3).reshape(64, 4096)

    return blocks(solution), blocks(residual)


def solution(mesh):
    return jax.shard_map(
        local,
        mesh=mesh,
        in_specs=(P(AX, None), P(AX), P(AX, None)),
        out_specs=(P(AX, None), P(AX, None)),
        check_vma=False,
    )
```

```python
import functools

import jax
import jax.numpy as jnp
from jax import lax
from jax.experimental import pallas as pl
from jax.experimental.pallas import tpu as pltpu
from jax.sharding import PartitionSpec as P

AX = ("sec", "blk")
N_BLK = 64
FAM = 8
WEIGHT = 0.8 / 6.0
PAD_ROWS = 34 * 64
SWEEP = 16
RESIDUE = 8
CONVERT = 8
F32 = jnp.float32
VMEM = pl.BlockSpec(memory_space=pltpu.VMEM)
SMEM = pl.BlockSpec(memory_space=pltpu.SMEM)
HBM = pl.BlockSpec(memory_space=pltpu.HBM)


def swap_pairs(unit, color):
    pairs, used = [], set()
    for b in range(N_BLK - unit):
        if (b // unit) % 2 == color:
            for s in (0, N_BLK):
                pairs += [(s + b, s + b + unit), (s + b + unit, s + b)]
            used |= {b, b + unit}
    for b in range(N_BLK):
        if b not in used:
            pairs += [(b, N_BLK + b), (N_BLK + b, b)]
    return pairs


def level_pairs():
    own, down, up = [], [], []
    for b in range(N_BLK):
        c, beyond = N_BLK + b, N_BLK + (b + 1) % N_BLK
        own += [(b, c), (c, b)]
        down += [(b, beyond), (c, b)]
        up += [(beyond, b), (b, c)]
    return own, down, up


UNITS = (16, 4, 1)
ORDER = (4, 5, 2, 3, 0, 1)
HALO_PAIRS = [swap_pairs(unit, color) for unit in UNITS for color in (0, 1)]
OWN_PAIRS, DOWN_PAIRS, UP_PAIRS = level_pairs()


def swap(x, pairs):
    return lax.ppermute(x, AX, pairs)


def position():
    return lax.axis_index("sec"), lax.axis_index("blk")


def parities(blk):
    return [(blk >> 4) & 1, (blk >> 2) & 1, blk & 1]


def lane_parts():
    lane = lax.broadcasted_iota(jnp.int32, (8, 128), 1)
    return lane >> 4, lane & 15


def roll(x, by):
    return pltpu.roll(x, by, 1)


def rows(ref, start, size=8):
    return ref[pl.ds(pl.multiple_of(start, 8), size), :]


def put(ref, start, value):
    ref[pl.ds(pl.multiple_of(start, 8), value.shape[0]), :] = value


def plane(ref, x):
    base = (x + 1) * 64
    return [[rows(ref, base + (q * 2 + oz) * 8) for oz in range(2)] for q in range(4)]


def around(a, below, above, j, k, hy=None, hz=None):
    zero = jnp.zeros((8, 128), F32)
    if hy is None:
        hy = [[zero, zero], [zero, zero]]
    if hz is None:
        hz = [[zero, zero] for _ in range(4)]
    y_low = [jnp.where(j == 0, hy[0][p], roll(a[3][p], 16)) for p in range(2)]
    y_high = [jnp.where(j == 7, hy[1][p], roll(a[0][p], 112)) for p in range(2)]
    total = []
    for r in range(4):
        z_low = jnp.where(k == 0, hz[r][0], roll(a[r][1], 1))
        z_high = jnp.where(k == 15, hz[r][1], roll(a[r][0], 127))
        line = []
        for p in range(2):
            y_sum = (a[r - 1][p] if r else y_low[p]) + (a[r + 1][p] if r < 3 else y_high[p])
            z_sum = a[r][1 - p] + (z_high if p else z_low)
            line.append((y_sum + z_sum) + (below[r][p] + above[r][p]))
        total.append(line)
    return total


def exchange(a, b, bit, partner):
    moved = jnp.take_along_axis(jnp.where(bit, a, b), partner, axis=1)
    return jnp.where(bit, moved, a), jnp.where(bit, b, moved)


def lane_bits(j, k):
    lane = j * 16 + k
    return [((lane & m) != 0, lane ^ m) for m in (1, 16, 32)]


def spread_index(j, k):
    return ((j & 1) * 4 + (j >> 1)) * 16 + 2 * (k & 7) + (k >> 3)


def to_working(v, j, k):
    z_bit, y_bit, y_next = lane_bits(j, k)
    s = [exchange(v[q][0], v[q][1], *z_bit) for q in range(4)]
    index = spread_index(j, k)
    result = [[None, None] for _ in range(4)]
    for p in range(2):
        t = [exchange(s[2 * h][p], s[2 * h + 1][p], *y_bit) for h in range(2)]
        for low in range(2):
            pair = exchange(t[0][low], t[1][low], *y_next)
            for high in range(2):
                result[low + 2 * high][p] = jnp.take_along_axis(pair[high], index, axis=1)
    return result


def to_given(a, j, k):
    z_bit, y_bit, y_next = lane_bits(j, k)
    index = (2 * (j & 3) + (j >> 2)) * 16 + (k >> 1) + 8 * (k & 1)
    s = [[None, None] for _ in range(4)]
    for p in range(2):
        t = [[None, None], [None, None]]
        for low in range(2):
            pair = [jnp.take_along_axis(a[low + 2 * high][p], index, axis=1) for high in range(2)]
            t[0][low], t[1][low] = exchange(pair[0], pair[1], *y_next)
        for h in range(2):
            s[2 * h][p], s[2 * h + 1][p] = exchange(t[h][0], t[h][1], *y_bit)
    return [exchange(s[q][0], s[q][1], *z_bit) for q in range(4)]


def given_rows(x, q, oz):
    octant = (x >> 4) * 4 + (q // 2) * 2 + oz
    return pl.ds(((x & 15) * 2 + q % 2) * 8 + octant, 8, stride=256)


def given_plane(ref, x):
    return [[ref[given_rows(x, q, oz), :] for oz in range(2)] for q in range(4)]


def put_given(ref, x, v):
    for q in range(4):
        for oz in range(2):
            ref[given_rows(x, q, oz), :] = v[q][oz]


def half_copies(source, target, sems, half):
    parts = [pl.ds(f * 256 + half * 128, 128) for f in range(FAM)]
    return [pltpu.make_async_copy(source.at[at], target.at[at], sems.at[half, f]) for f, at in enumerate(parts)]


def put_plane(ref, x, a):
    for r in range(4):
        for p in range(2):
            put(ref, (x + 1) * 64 + (r * 2 + p) * 8, a[r][p])


def clear_pads(ref):
    for start in (0, 33 * 64):
        ref[start : start + 64, :] = jnp.zeros((64, 128), F32)


def smooth(rhs, mid, emit):
    j, k = lane_parts()
    clear_pads(rhs)
    clear_pads(mid)

    def sweep(src, write):
        def body(i, _):
            x0 = i * SWEEP
            p = [plane(src, x0 + m - 1) for m in range(SWEEP + 2)]
            result = [around(p[m + 1], p[m], p[m + 2], j, k) for m in range(SWEEP)]
            for m in range(SWEEP):
                for r in range(4):
                    for c in range(2):
                        write((x0 + m + 1) * 64 + (r * 2 + c) * 8, p[m + 1][r][c], result[m][r][c])
            return 0

        lax.fori_loop(0, 32 // SWEEP, body, 0)

    def first(at, a, m):
        put(mid, at, 1.2 * a + WEIGHT * m)

    def second(at, a, m):
        emit(at, WEIGHT * (rows(rhs, at) + 0.2 * a + WEIGHT * m))

    sweep(rhs, first)
    sweep(mid, second)


def put_down(down, i, pair):
    for r in range(2):
        put(down, (r * 16 + i) * 8, pair[r])


def restrict_pair(a, b):
    c = [[a[r][p] + b[r][p] for p in range(2)] for r in range(4)]
    return [0.5 * ((c[2 * r][0] + c[2 * r][1]) + (c[2 * r + 1][0] + c[2 * r + 1][1])) for r in range(2)]


def restrict_given(a, b, j, k):
    z_even, y_even = (k & 1) == 0, (j & 1) == 0
    u = []
    for q in range(4):
        lo, hi = a[q][0] + b[q][0], a[q][1] + b[q][1]
        u.append(jnp.where(z_even, lo + roll(lo, 127), hi + roll(hi, 1)))
    m = []
    for h in range(2):
        m.append(jnp.where(y_even, u[2 * h] + roll(u[2 * h], 112), u[2 * h + 1] + roll(u[2 * h + 1], 16)))
    index = spread_index(j, k)
    return [0.5 * jnp.take_along_axis(n, index, axis=1) for n in exchange(m[0], m[1], *lane_bits(j, k)[2])]


def parent_slots(parent, blk):
    own_count, next_count = jnp.int32(0), jnp.int32(0)
    found = []
    for g in range(FAM):
        value = parent[g]
        chip = (value >> 6) - N_BLK
        to_own = (value >= 0) & (chip == blk)
        to_next = (value >= 0) & (chip == ((blk + 1) & (N_BLK - 1)))
        found.append((to_own, to_next, own_count, next_count, value & 63))
        own_count = own_count + to_own.astype(jnp.int32)
        next_count = next_count + to_next.astype(jnp.int32)
    return found


def send_down(down, parent, blk, own, nxt, tags):
    for buf in (own, nxt):
        if tags:
            buf[128:136, :] = jnp.full((8, 128), -1.0, F32)
    for g, (to_own, to_next, own_slot, next_slot, block) in enumerate(parent_slots(parent, blk)):
        for going, slot, buf in ((to_own, own_slot, own), (to_next, next_slot, nxt)):

            @pl.when(going)
            def _(slot=slot, buf=buf, block=block, g=g):
                put(buf, slot * 32, down[pl.ds(g, 32, stride=8), :])
                if tags:
                    buf[pl.ds(128 + slot, 1), :] = jnp.full((1, 128), block.astype(F32), F32)


def block_place(block, s, half):
    f, o = block >> 3, block & 7
    start = ((o >> 2) * 16 + 8 * half + 1) * 64 + f
    at = [[pl.ds(start + ((2 * t + s) * 2 + p) * 8, 8, stride=64) for p in range(2)] for t in range(2)]
    return at, (o >> 1) & 1, o & 1


def add_incoming(rhs, tags, arrived):
    j, k = lane_parts()
    index = [[(2 * (j & 3) + t) * 16 + 2 * (k & 7) + p for p in range(2)] for t in range(2)]
    for n in range(8):
        buf, slot, tag = arrived[n // 4], n % 4, tags[n]

        used, block = tag >= 0, jnp.maximum(tag, 0)
        places, spread = [], []
        for s in range(2):
            for half in range(2):
                at, oy, oz = block_place(block, s, half)
                here = ((j >> 2) == jnp.where(used, oy, -1)) & ((k >> 3) == oz)
                value = rows(buf, slot * 32 + s * 16 + half * 8)
                for t in range(2):
                    for p in range(2):
                        places.append(at[t][p])
                        spread.append(jnp.where(here, jnp.take_along_axis(value, index[t][p], axis=1), 0.0))
        total = [rhs[at, :] + value for at, value in zip(places, spread)]
        for at, value in zip(places, total):
            rhs[at, :] = value


def answer(correction, tags, out):
    j, k = lane_parts()
    y_odd, z_odd = (j & 1) == 1, (k & 1) == 1
    for n in range(8):
        buf, slot, tag = out[n // 4], n % 4, tags[n]

        block = jnp.maximum(tag, 0)
        found = []
        for s in range(2):
            for half in range(2):
                at, oy, oz = block_place(block, s, half)
                index = (4 * oy + (j >> 1)) * 16 + 8 * oz + (k >> 1)
                v = [[jnp.take_along_axis(correction[at[t][p], :], index, axis=1) for p in range(2)] for t in range(2)]
                v = [jnp.where(z_odd, v[t][1], v[t][0]) for t in range(2)]
                found.append(jnp.where(y_odd, v[1], v[0]))
        for i, value in enumerate(found):
            put(buf, slot * 32 + i * 8, value)


def unload_half(source, given, out, sems, half):
    j, k = lane_parts()

    def convert(n, _):
        first = 16 * n + 8 * half
        planes = [to_given(plane(source, first + m), j, k) for m in range(8)]
        for m in range(8):
            put_given(given, first + m, planes[m])
        return 0

    lax.fori_loop(0, 2, convert, 0)
    for copy in half_copies(given, out, sems, half):
        copy.start()


def finish_unload(given, out, sems):
    for half in range(2):
        for copy in half_copies(given, out, sems, half):
            copy.wait()


def first_down_kernel(parent, tiles, nxt, own, down, source, places, sems, place_sem):
    sec, blk = position()
    j, k = lane_parts()

    @pl.when(sec == 0)
    def _():
        halves = [half_copies(tiles, source, sems, half) for half in range(2)]
        place = pltpu.make_async_copy(parent, places, place_sem)
        for copy in (*halves[0], *halves[1], place):
            copy.start()

        def pair(i):
            return restrict_given(given_plane(source, 2 * i), given_plane(source, 2 * i + 1), j, k)

        for half in range(2):
            for copy in halves[half]:
                copy.wait()

            def pairs(n, _):
                first = 8 * n + 4 * half
                done = [pair(first + m) for m in range(4)]
                for m in range(4):
                    put_down(down, first + m, done[m])
                return 0

            lax.fori_loop(0, 2, pairs, 0, unroll=True)
        place.wait()
        send_down(down, places, blk, own, nxt, True)


def load_kernel(source, src, sol, mid):
    sec, _ = position()

    j, k = lane_parts()

    def convert(i, _):
        planes = [to_working(given_plane(source, CONVERT * i + m), j, k) for m in range(CONVERT)]
        for m in range(CONVERT):
            put_plane(src, CONVERT * i + m, planes[m])
        return 0

    lax.fori_loop(0, 32 // CONVERT, convert, 0)

    @pl.when(sec == 0)
    def _():
        def emit(at, value):
            put(sol, at, value)

        smooth(src, mid, emit)


def coarse_kernel(first, *refs):
    if first:
        res, in_next, in_own, out_sol, out_next, out_own, tags, rhs, mid, smem, sem = refs
    else:
        tags, res, sol, _, in_next, in_own, out_sol, out_next, out_own, rhs, mid, corr = refs
    sec, _ = position()

    if first:
        for j in range(8):
            tags[j] = jnp.int32(-1)

    @pl.when(sec == 1)
    def _():
        if first:
            copies = [
                pltpu.make_async_copy(buf.at[128:136, :], smem.at[k], sem.at[k])
                for k, buf in enumerate((in_own, in_next))
            ]
            for c in copies:
                c.start()

        def copy(i, _):
            put(rhs, i * 64, rows(res, i * 64, 64))
            return 0

        lax.fori_loop(1, 33, copy, 0)
        if first:
            for k, c in enumerate(copies):
                c.wait()
                for j in range(4):
                    tags[k * 4 + j] = smem[k, j, 0].astype(jnp.int32)
        add_incoming(rhs, tags, (in_own, in_next))

        def emit(at, value):
            if first:
                put(out_sol, at, value)
            else:
                put(corr, at, value)
                put(out_sol, at, rows(sol, at) + value)

        smooth(rhs, mid, emit)
        answer(out_sol if first else corr, tags, (out_own, out_next))


def lift_kernel(parent, sol, coarse_sol, in_next, in_own, out_sol, *refs):
    out, (lift, face) = refs[:6], refs[6:]
    sec, blk = position()
    j, k = lane_parts()

    def pack(make, g, _):
        planes = make(g)
        zero = jnp.zeros((8, 128), F32)
        y_low, y_high, z_low, z_high = [zero] * 2, [zero] * 2, [zero] * 4, [zero] * 4
        for m, a in enumerate(planes):
            y_mask, z_mask = j == m, k == m
            for p in range(2):
                y_low[p] = jnp.where(y_mask, roll(a[0][p], 16 * m), y_low[p])
                y_high[p] = jnp.where(y_mask, roll(a[3][p], (16 * m + 16) % 128), y_high[p])
            for r in range(4):
                z_low[r] = jnp.where(z_mask, roll(a[r][0], m), z_low[r])
                z_high[r] = jnp.where(z_mask, roll(a[r][1], (m + 113) % 128), z_high[r])
        for m, a in enumerate(planes):
            put_plane(out_sol, 8 * g + m, a)
        for o in range(2):
            put(face, 128 + (o * 4 + g) * 8, y_low[o])
            put(face, 192 + (o * 4 + g) * 8, y_high[o])
        half = g & 1
        here = (k >> 3) == half
        for q in range(4):
            at = 256 + (q * 2 + (g >> 1)) * 8
            put(face, at, jnp.where(here, roll(z_low[q], 8 * half), rows(face, at)))
            put(face, at + 64, jnp.where(here, roll(z_high[q], 8 * half), rows(face, at + 64)))
        return 0

    @pl.when(sec == 0)
    def _():
        for g, (to_own, to_next, own_slot, next_slot, _) in enumerate(parent_slots(parent, blk)):
            at = pl.ds(g, 32, stride=8)

            @pl.when(to_own)
            def _(at=at, slot=own_slot):
                lift[at, :] = rows(in_own, slot * 32, 32)

            @pl.when(to_next)
            def _(at=at, slot=next_slot):
                lift[at, :] = rows(in_next, slot * 32, 32)

            @pl.when(jnp.logical_not(to_own | to_next))
            def _(at=at):
                lift[at, :] = jnp.zeros((32, 128), F32)

        def lifted(g):
            planes = [plane(sol, 8 * g + m) for m in range(8)]
            for m in range(4):
                for s in range(2):
                    value = rows(lift, (s * 16 + 4 * g + m) * 8)
                    for x in (2 * m, 2 * m + 1):
                        for r in (2 * s, 2 * s + 1):
                            planes[x][r] = [planes[x][r][p] + value for p in range(2)]
            return planes

        lax.fori_loop(0, 4, functools.partial(pack, lifted), 0, unroll=True)

    @pl.when(sec == 1)
    def _():
        lax.fori_loop(0, 4, functools.partial(pack, lambda g: [plane(coarse_sol, 8 * g + m) for m in range(8)]), 0, unroll=True)

    put(face, 0, rows(out_sol, 64, 64))
    put(face, 64, rows(out_sol, 32 * 64, 64))
    for axis, parity in enumerate(parities(blk)):
        for color in range(2):
            d = 2 * axis + (parity == color).astype(jnp.int32)
            out[ORDER.index(2 * axis + color)][...] = rows(face, d * 64, 64)


def residual_kernel(level, parent, neighbor, src, sol, *refs):
    sent, got = ([refs[first + ORDER.index(n)] for n in range(6)] for first in (0, 6))
    last, fine = level is None, level == 0
    if fine:
        res, nxt, own, halo, table, down = refs[12:]
    elif last:
        out, halo, table, res, given, sems = refs[12:]
    else:
        res, halo, table = refs[12:]
    sec, blk = position()

    def whole():
        j, k = lane_parts()

        for axis, parity in enumerate(parities(blk)):
            for color in range(2):
                odd = (parity == color).astype(jnp.int32)
                put(table, (2 * axis + 1 - odd) * 128, sent[2 * axis + color][...])
                put(table, (2 * axis + odd) * 128 + 64, got[2 * axis + color][...])
        device = sec * N_BLK + blk

        def gather(g, _):
            for d in range(6):
                other = neighbor[g, d]
                local = (other >> 3) == device
                start = d * 128 + jnp.where(local, 0, 64) + (other & 7)
                value = table[pl.ds(start, 8, stride=8), :]
                halo[pl.ds(d * 64 + g, 8, stride=8), :] = jnp.where(other >= 0, value, 0.0)
            return 0

        lax.fori_loop(0, FAM, gather, 0)

        def side(base):
            return [[rows(halo, base + (q * 2 + o) * 8) for o in range(2)] for q in range(4)]

        def residue(x, a, below, above):
            y_at, z_at = x & 7, x & 15
            y_rows = [128 + (o * 4 + (x >> 3)) * 8 for o in range(2)]
            hy = [
                [roll(rows(halo, y_rows[o]), (128 - 16 * y_at) & 127) for o in range(2)],
                [roll(rows(halo, y_rows[o] + 64), 112 - 16 * y_at) for o in range(2)],
            ]
            hz = []
            for q in range(4):
                at = 256 + (q * 2 + (x >> 4)) * 8
                hz.append([roll(rows(halo, at), (128 - z_at) & 127), roll(rows(halo, at + 64), 15 - z_at)])
            m = around(a, below, above, j, k, hy, hz)
            s = plane(src, x)
            return [[s[q][o] - 6.0 * a[q][o] + m[q][o] for o in range(2)] for q in range(4)]

        def group(x):
            p = [side(0) if x == 0 else plane(sol, x - 1)]
            p += [plane(sol, x + m) for m in range(RESIDUE)]
            p.append(side(64) if x + RESIDUE == 32 else plane(sol, x + RESIDUE))
            r = [residue(x + m, p[m + 1], p[m], p[m + 2]) for m in range(RESIDUE)]
            for m in range(RESIDUE):
                put_plane(res, x + m, r[m])
            if fine:
                for m in range(0, RESIDUE, 2):
                    put_down(down, (x + m) // 2, restrict_pair(r[m], r[m + 1]))

        for half in range(2):
            for x in range(8 * half, 32, 16):
                for first in range(x, x + 8, RESIDUE):
                    group(first)
            if last:
                unload_half(res, given, out, sems, half)
        if last:
            finish_unload(given, out, sems)
        if fine:
            send_down(down, parent, blk, own, nxt, False)

    if last:
        whole()
    else:
        pl.when(sec == level)(whole)


def fine_kernel(res, sol, out_sol, rhs, mid):
    sec, _ = position()

    @pl.when(sec == 0)
    def _():
        def copy(i, _):
            put(rhs, i * 64, rows(res, i * 64, 64))
            return 0

        lax.fori_loop(1, 33, copy, 0)

        def emit(at, value):
            put(out_sol, at, rows(sol, at) + value)

        smooth(rhs, mid, emit)


def unload_kernel(sol, out, given, sems):
    for half in range(2):
        unload_half(sol, given, out, sems, half)
    finish_unload(given, out, sems)


def shape(n, dtype=F32):
    return jax.ShapeDtypeStruct((n, 128), dtype)


def scratch(n):
    return pltpu.VMEM((n, 128), F32)


def call(kernel, name, in_specs, out_shape, scratch_shapes=(), out_specs=None):
    return pl.pallas_call(
        kernel,
        name=name,
        in_specs=in_specs,
        out_shape=out_shape,
        out_specs=out_specs or [VMEM] * len(out_shape),
        scratch_shapes=list(scratch_shapes),
        compiler_params=pltpu.CompilerParams(vmem_limit_bytes=32 << 20),
    )


def local(source, parent, neighbor):
    tiles = source.reshape(FAM, 8, 32, 128).transpose(0, 2, 1, 3).reshape(2048, 128)
    here = pltpu.with_memory_space_constraint(tiles, pltpu.HBM)
    place = pltpu.with_memory_space_constraint(parent, pltpu.HBM)
    pad, pads = shape(PAD_ROWS), scratch(PAD_ROWS)

    def both(nxt, own, pairs):
        return swap(nxt, pairs), swap(own, OWN_PAIRS)

    nxt, own = call(
        first_down_kernel,
        "first_down",
        [HBM, HBM],
        (shape(136), shape(136)),
        [
            scratch(256),
            scratch(2048),
            pltpu.SMEM((FAM,), jnp.int32),
            pltpu.SemaphoreType.DMA((2, FAM)),
            pltpu.SemaphoreType.DMA,
        ],
    )(place, here)
    got_next, got_own = both(nxt, own, DOWN_PAIRS)
    src, fine_sol = call(load_kernel, "load", [VMEM], (pad, pad), [pads])(tiles)
    coarse_sol, nxt, own, tags = call(
        functools.partial(coarse_kernel, True),
        "coarse_0",
        [VMEM] * 3,
        (pad, shape(128), shape(128), jax.ShapeDtypeStruct((8,), jnp.int32)),
        [pads, pads, pltpu.SMEM((2, 8, 128), F32), pltpu.SemaphoreType.DMA((2,))],
        [VMEM, VMEM, VMEM, SMEM],
    )(src, got_next, got_own)

    def lift_and_share(n, nxt, own):
        got_next, got_own = both(nxt, own, UP_PAIRS)
        out = call(
            lift_kernel,
            f"lift_{n}",
            [SMEM] + [VMEM] * 4,
            (pad,) + (shape(64),) * 6,
            [scratch(256), scratch(384)],
        )(parent, fine_sol, coarse_sol, got_next, got_own)
        sol, sent = out[0], out[1:]
        return sol, [*sent, *(swap(face, HALO_PAIRS[n]) for face, n in zip(sent, ORDER))]

    def residue_of(level, name, sol, faces, out_shape, more=(), out_specs=None):
        return call(
            functools.partial(residual_kernel, level),
            name,
            [SMEM, SMEM] + [VMEM] * 14,
            out_shape,
            [scratch(384), scratch(768), *more],
            out_specs,
        )(parent, neighbor, src, sol, *faces)

    sol, faces = lift_and_share(0, nxt, own)
    res, nxt, own = residue_of(0, "residue_fine", sol, faces, (pad, shape(128), shape(128)), [scratch(256)])
    got_next, got_own = both(nxt, own, DOWN_PAIRS)
    (coarse_res,) = residue_of(1, "residue_coarse", sol, faces, (pad,))
    (fine_sol,) = call(fine_kernel, "fine", [VMEM, VMEM], (pad,), [pads, pads])(res, sol)
    coarse_sol, nxt, own = call(
        functools.partial(coarse_kernel, False),
        "coarse_1",
        [SMEM] + [VMEM] * 5,
        (pad, shape(128), shape(128)),
        [pads, pads, pads],
    )(tags, coarse_res, sol, fine_sol, got_next, got_own)
    sol, faces = lift_and_share(1, nxt, own)
    leave = [scratch(2048), pltpu.SemaphoreType.DMA((2, FAM))]
    (solution,) = call(unload_kernel, "unload", [VMEM], (shape(2048),), leave, [HBM])(sol)
    (residual,) = residue_of(None, "residual", sol, faces, (shape(2048),), [pads, *leave], [HBM])

    def blocks(x):
        return x.reshape(FAM, 32, 8, 128).transpose(0, 2, 1, 3).reshape(64, 4096)

    return blocks(solution), blocks(residual)


def solution(mesh):
    return jax.shard_map(
        local,
        mesh=mesh,
        in_specs=(P(AX, None), P(AX), P(AX, None)),
        out_specs=(P(AX, None), P(AX, None)),
        check_vma=False,
    )
```

```python
import functools

import jax
import jax.numpy as jnp
from jax import lax
from jax.experimental import pallas as pl
from jax.experimental.pallas import tpu as pltpu
from jax.sharding import PartitionSpec as P

AX = ("sec", "blk")
N_BLK = 64
FAM = 8
WEIGHT = 0.8 / 6.0
PAD_ROWS = 34 * 64
SWEEP = 16
RESIDUE = 8
CONVERT = 8
F32 = jnp.float32
VMEM = pl.BlockSpec(memory_space=pltpu.VMEM)
SMEM = pl.BlockSpec(memory_space=pltpu.SMEM)
HBM = pl.BlockSpec(memory_space=pltpu.HBM)


def swap_pairs(unit, color):
    pairs, used = [], set()
    for b in range(N_BLK - unit):
        if (b // unit) % 2 == color:
            for s in (0, N_BLK):
                pairs += [(s + b, s + b + unit), (s + b + unit, s + b)]
            used |= {b, b + unit}
    for b in range(N_BLK):
        if b not in used:
            pairs += [(b, N_BLK + b), (N_BLK + b, b)]
    return pairs


def level_pairs():
    own, down, up = [], [], []
    for b in range(N_BLK):
        c, beyond = N_BLK + b, N_BLK + (b + 1) % N_BLK
        own += [(b, c), (c, b)]
        down += [(b, beyond), (c, b)]
        up += [(beyond, b), (b, c)]
    return own, down, up


UNITS = (16, 4, 1)
ORDER = (4, 5, 3, 2, 0, 1)
HALO_PAIRS = [swap_pairs(unit, color) for unit in UNITS for color in (0, 1)]
OWN_PAIRS, DOWN_PAIRS, UP_PAIRS = level_pairs()


def swap(x, pairs):
    return lax.ppermute(x, AX, pairs)


def position():
    return lax.axis_index("sec"), lax.axis_index("blk")


def parities(blk):
    return [(blk >> 4) & 1, (blk >> 2) & 1, blk & 1]


def lane_parts():
    lane = lax.broadcasted_iota(jnp.int32, (8, 128), 1)
    return lane >> 4, lane & 15


def roll(x, by):
    return pltpu.roll(x, by, 1)


def rows(ref, start, size=8):
    return ref[pl.ds(pl.multiple_of(start, 8), size), :]


def put(ref, start, value):
    ref[pl.ds(pl.multiple_of(start, 8), value.shape[0]), :] = value


def plane(ref, x):
    base = (x + 1) * 64
    return [[rows(ref, base + (q * 2 + oz) * 8) for oz in range(2)] for q in range(4)]


def around(a, below, above, j, k, hy=None, hz=None):
    zero = jnp.zeros((8, 128), F32)
    if hy is None:
        hy = [[zero, zero], [zero, zero]]
    if hz is None:
        hz = [[zero, zero] for _ in range(4)]
    y_low = [jnp.where(j == 0, hy[0][p], roll(a[3][p], 16)) for p in range(2)]
    y_high = [jnp.where(j == 7, hy[1][p], roll(a[0][p], 112)) for p in range(2)]
    total = []
    for r in range(4):
        z_low = jnp.where(k == 0, hz[r][0], roll(a[r][1], 1))
        z_high = jnp.where(k == 15, hz[r][1], roll(a[r][0], 127))
        line = []
        for p in range(2):
            y_sum = (a[r - 1][p] if r else y_low[p]) + (a[r + 1][p] if r < 3 else y_high[p])
            z_sum = a[r][1 - p] + (z_high if p else z_low)
            line.append((y_sum + z_sum) + (below[r][p] + above[r][p]))
        total.append(line)
    return total


def exchange(a, b, bit, partner):
    moved = jnp.take_along_axis(jnp.where(bit, a, b), partner, axis=1)
    return jnp.where(bit, moved, a), jnp.where(bit, b, moved)


def lane_bits(j, k):
    lane = j * 16 + k
    return [((lane & m) != 0, lane ^ m) for m in (1, 16, 32)]


def spread_index(j, k):
    return ((j & 1) * 4 + (j >> 1)) * 16 + 2 * (k & 7) + (k >> 3)


def to_working(v, j, k):
    z_bit, y_bit, y_next = lane_bits(j, k)
    s = [exchange(v[q][0], v[q][1], *z_bit) for q in range(4)]
    index = spread_index(j, k)
    result = [[None, None] for _ in range(4)]
    for p in range(2):
        t = [exchange(s[2 * h][p], s[2 * h + 1][p], *y_bit) for h in range(2)]
        for low in range(2):
            pair = exchange(t[0][low], t[1][low], *y_next)
            for high in range(2):
                result[low + 2 * high][p] = jnp.take_along_axis(pair[high], index, axis=1)
    return result


def to_given(a, j, k):
    z_bit, y_bit, y_next = lane_bits(j, k)
    index = (2 * (j & 3) + (j >> 2)) * 16 + (k >> 1) + 8 * (k & 1)
    s = [[None, None] for _ in range(4)]
    for p in range(2):
        t = [[None, None], [None, None]]
        for low in range(2):
            pair = [jnp.take_along_axis(a[low + 2 * high][p], index, axis=1) for high in range(2)]
            t[0][low], t[1][low] = exchange(pair[0], pair[1], *y_next)
        for h in range(2):
            s[2 * h][p], s[2 * h + 1][p] = exchange(t[h][0], t[h][1], *y_bit)
    return [exchange(s[q][0], s[q][1], *z_bit) for q in range(4)]


def given_rows(x, q, oz):
    octant = (x >> 4) * 4 + (q // 2) * 2 + oz
    return pl.ds(((x & 15) * 2 + q % 2) * 8 + octant, 8, stride=256)


def given_plane(ref, x):
    return [[ref[given_rows(x, q, oz), :] for oz in range(2)] for q in range(4)]


def put_given(ref, x, v):
    for q in range(4):
        for oz in range(2):
            ref[given_rows(x, q, oz), :] = v[q][oz]


def half_copies(source, target, sems, half):
    parts = [pl.ds(f * 256 + half * 128, 128) for f in range(FAM)]
    return [pltpu.make_async_copy(source.at[at], target.at[at], sems.at[half, f]) for f, at in enumerate(parts)]


def put_plane(ref, x, a):
    for r in range(4):
        for p in range(2):
            put(ref, (x + 1) * 64 + (r * 2 + p) * 8, a[r][p])


def clear_pads(ref):
    for start in (0, 33 * 64):
        ref[start : start + 64, :] = jnp.zeros((64, 128), F32)


def smooth(rhs, mid, emit):
    j, k = lane_parts()
    clear_pads(rhs)
    clear_pads(mid)

    def sweep(src, write):
        def body(i, _):
            x0 = i * SWEEP
            p = [plane(src, x0 + m - 1) for m in range(SWEEP + 2)]
            result = [around(p[m + 1], p[m], p[m + 2], j, k) for m in range(SWEEP)]
            for m in range(SWEEP):
                for r in range(4):
                    for c in range(2):
                        write((x0 + m + 1) * 64 + (r * 2 + c) * 8, p[m + 1][r][c], result[m][r][c])
            return 0

        lax.fori_loop(0, 32 // SWEEP, body, 0)

    def first(at, a, m):
        put(mid, at, 1.2 * a + WEIGHT * m)

    def second(at, a, m):
        emit(at, WEIGHT * (rows(rhs, at) + 0.2 * a + WEIGHT * m))

    sweep(rhs, first)
    sweep(mid, second)


def put_down(down, i, pair):
    for r in range(2):
        put(down, (r * 16 + i) * 8, pair[r])


def restrict_pair(a, b):
    c = [[a[r][p] + b[r][p] for p in range(2)] for r in range(4)]
    return [0.5 * ((c[2 * r][0] + c[2 * r][1]) + (c[2 * r + 1][0] + c[2 * r + 1][1])) for r in range(2)]


def restrict_given(a, b, j, k):
    z_even, y_even = (k & 1) == 0, (j & 1) == 0
    u = []
    for q in range(4):
        lo, hi = a[q][0] + b[q][0], a[q][1] + b[q][1]
        u.append(jnp.where(z_even, lo + roll(lo, 127), hi + roll(hi, 1)))
    m = []
    for h in range(2):
        m.append(jnp.where(y_even, u[2 * h] + roll(u[2 * h], 112), u[2 * h + 1] + roll(u[2 * h + 1], 16)))
    index = spread_index(j, k)
    return [0.5 * jnp.take_along_axis(n, index, axis=1) for n in exchange(m[0], m[1], *lane_bits(j, k)[2])]


def parent_slots(parent, blk):
    own_count, next_count = jnp.int32(0), jnp.int32(0)
    found = []
    for g in range(FAM):
        value = parent[g]
        chip = (value >> 6) - N_BLK
        to_own = (value >= 0) & (chip == blk)
        to_next = (value >= 0) & (chip == ((blk + 1) & (N_BLK - 1)))
        found.append((to_own, to_next, own_count, next_count, value & 63))
        own_count = own_count + to_own.astype(jnp.int32)
        next_count = next_count + to_next.astype(jnp.int32)
    return found


def send_down(down, parent, blk, own, nxt, tags):
    for buf in (own, nxt):
        if tags:
            buf[128:136, :] = jnp.full((8, 128), -1.0, F32)
    for g, (to_own, to_next, own_slot, next_slot, block) in enumerate(parent_slots(parent, blk)):
        for going, slot, buf in ((to_own, own_slot, own), (to_next, next_slot, nxt)):

            @pl.when(going)
            def _(slot=slot, buf=buf, block=block, g=g):
                put(buf, slot * 32, down[pl.ds(g, 32, stride=8), :])
                if tags:
                    buf[pl.ds(128 + slot, 1), :] = jnp.full((1, 128), block.astype(F32), F32)


def block_place(block, s, half):
    f, o = block >> 3, block & 7
    start = ((o >> 2) * 16 + 8 * half + 1) * 64 + f
    at = [[pl.ds(start + ((2 * t + s) * 2 + p) * 8, 8, stride=64) for p in range(2)] for t in range(2)]
    return at, (o >> 1) & 1, o & 1


def add_incoming(rhs, tags, arrived):
    j, k = lane_parts()
    index = [[(2 * (j & 3) + t) * 16 + 2 * (k & 7) + p for p in range(2)] for t in range(2)]
    for n in range(8):
        buf, slot, tag = arrived[n // 4], n % 4, tags[n]

        used, block = tag >= 0, jnp.maximum(tag, 0)
        places, spread = [], []
        for s in range(2):
            for half in range(2):
                at, oy, oz = block_place(block, s, half)
                here = ((j >> 2) == jnp.where(used, oy, -1)) & ((k >> 3) == oz)
                value = rows(buf, slot * 32 + s * 16 + half * 8)
                for t in range(2):
                    for p in range(2):
                        places.append(at[t][p])
                        spread.append(jnp.where(here, jnp.take_along_axis(value, index[t][p], axis=1), 0.0))
        total = [rhs[at, :] + value for at, value in zip(places, spread)]
        for at, value in zip(places, total):
            rhs[at, :] = value


def answer(correction, tags, out):
    j, k = lane_parts()
    y_odd, z_odd = (j & 1) == 1, (k & 1) == 1
    for n in range(8):
        buf, slot, tag = out[n // 4], n % 4, tags[n]

        block = jnp.maximum(tag, 0)
        found = []
        for s in range(2):
            for half in range(2):
                at, oy, oz = block_place(block, s, half)
                index = (4 * oy + (j >> 1)) * 16 + 8 * oz + (k >> 1)
                v = [[jnp.take_along_axis(correction[at[t][p], :], index, axis=1) for p in range(2)] for t in range(2)]
                v = [jnp.where(z_odd, v[t][1], v[t][0]) for t in range(2)]
                found.append(jnp.where(y_odd, v[1], v[0]))
        for i, value in enumerate(found):
            put(buf, slot * 32 + i * 8, value)


def unload_half(source, given, out, sems, half):
    j, k = lane_parts()

    def convert(n, _):
        first = 16 * n + 8 * half
        planes = [to_given(plane(source, first + m), j, k) for m in range(8)]
        for m in range(8):
            put_given(given, first + m, planes[m])
        return 0

    lax.fori_loop(0, 2, convert, 0)
    for copy in half_copies(given, out, sems, half):
        copy.start()


def finish_unload(given, out, sems):
    for half in range(2):
        for copy in half_copies(given, out, sems, half):
            copy.wait()


def first_down_kernel(parent, tiles, nxt, own, down, source, places, sems, place_sem):
    sec, blk = position()
    j, k = lane_parts()

    @pl.when(sec == 0)
    def _():
        halves = [half_copies(tiles, source, sems, half) for half in range(2)]
        place = pltpu.make_async_copy(parent, places, place_sem)
        for copy in (*halves[0], *halves[1], place):
            copy.start()

        def pair(i):
            return restrict_given(given_plane(source, 2 * i), given_plane(source, 2 * i + 1), j, k)

        for half in range(2):
            for copy in halves[half]:
                copy.wait()

            def pairs(n, _):
                first = 8 * n + 4 * half
                done = [pair(first + m) for m in range(4)]
                for m in range(4):
                    put_down(down, first + m, done[m])
                return 0

            lax.fori_loop(0, 2, pairs, 0, unroll=True)
        place.wait()
        send_down(down, places, blk, own, nxt, True)


def load_kernel(source, src, sol, mid):
    sec, _ = position()

    j, k = lane_parts()

    def convert(i, _):
        planes = [to_working(given_plane(source, CONVERT * i + m), j, k) for m in range(CONVERT)]
        for m in range(CONVERT):
            put_plane(src, CONVERT * i + m, planes[m])
        return 0

    lax.fori_loop(0, 32 // CONVERT, convert, 0)

    @pl.when(sec == 0)
    def _():
        def emit(at, value):
            put(sol, at, value)

        smooth(src, mid, emit)


def coarse_kernel(first, *refs):
    if first:
        res, in_next, in_own, out_sol, out_next, out_own, tags, rhs, mid, smem, sem = refs
    else:
        tags, res, sol, _, in_next, in_own, out_sol, out_next, out_own, rhs, mid, corr = refs
    sec, _ = position()

    if first:
        for j in range(8):
            tags[j] = jnp.int32(-1)

    @pl.when(sec == 1)
    def _():
        if first:
            copies = [
                pltpu.make_async_copy(buf.at[128:136, :], smem.at[k], sem.at[k])
                for k, buf in enumerate((in_own, in_next))
            ]
            for c in copies:
                c.start()

        def copy(i, _):
            put(rhs, i * 64, rows(res, i * 64, 64))
            return 0

        lax.fori_loop(1, 33, copy, 0)
        if first:
            for k, c in enumerate(copies):
                c.wait()
                for j in range(4):
                    tags[k * 4 + j] = smem[k, j, 0].astype(jnp.int32)
        add_incoming(rhs, tags, (in_own, in_next))

        def emit(at, value):
            if first:
                put(out_sol, at, value)
            else:
                put(corr, at, value)
                put(out_sol, at, rows(sol, at) + value)

        smooth(rhs, mid, emit)
        answer(out_sol if first else corr, tags, (out_own, out_next))


def lift_kernel(parent, sol, coarse_sol, in_next, in_own, out_sol, *refs):
    out, (lift, face) = refs[:6], refs[6:]
    sec, blk = position()
    j, k = lane_parts()

    def pack(make, g, _):
        planes = make(g)
        zero = jnp.zeros((8, 128), F32)
        y_low, y_high, z_low, z_high = [zero] * 2, [zero] * 2, [zero] * 4, [zero] * 4
        for m, a in enumerate(planes):
            y_mask, z_mask = j == m, k == m
            for p in range(2):
                y_low[p] = jnp.where(y_mask, roll(a[0][p], 16 * m), y_low[p])
                y_high[p] = jnp.where(y_mask, roll(a[3][p], (16 * m + 16) % 128), y_high[p])
            for r in range(4):
                z_low[r] = jnp.where(z_mask, roll(a[r][0], m), z_low[r])
                z_high[r] = jnp.where(z_mask, roll(a[r][1], (m + 113) % 128), z_high[r])
        for m, a in enumerate(planes):
            put_plane(out_sol, 8 * g + m, a)
        for o in range(2):
            put(face, 128 + (o * 4 + g) * 8, y_low[o])
            put(face, 192 + (o * 4 + g) * 8, y_high[o])
        half = g & 1
        here = (k >> 3) == half
        for q in range(4):
            at = 256 + (q * 2 + (g >> 1)) * 8
            put(face, at, jnp.where(here, roll(z_low[q], 8 * half), rows(face, at)))
            put(face, at + 64, jnp.where(here, roll(z_high[q], 8 * half), rows(face, at + 64)))
        return 0

    @pl.when(sec == 0)
    def _():
        for g, (to_own, to_next, own_slot, next_slot, _) in enumerate(parent_slots(parent, blk)):
            at = pl.ds(g, 32, stride=8)

            @pl.when(to_own)
            def _(at=at, slot=own_slot):
                lift[at, :] = rows(in_own, slot * 32, 32)

            @pl.when(to_next)
            def _(at=at, slot=next_slot):
                lift[at, :] = rows(in_next, slot * 32, 32)

            @pl.when(jnp.logical_not(to_own | to_next))
            def _(at=at):
                lift[at, :] = jnp.zeros((32, 128), F32)

        def lifted(g):
            planes = [plane(sol, 8 * g + m) for m in range(8)]
            for m in range(4):
                for s in range(2):
                    value = rows(lift, (s * 16 + 4 * g + m) * 8)
                    for x in (2 * m, 2 * m + 1):
                        for r in (2 * s, 2 * s + 1):
                            planes[x][r] = [planes[x][r][p] + value for p in range(2)]
            return planes

        lax.fori_loop(0, 4, functools.partial(pack, lifted), 0, unroll=True)

    @pl.when(sec == 1)
    def _():
        lax.fori_loop(0, 4, functools.partial(pack, lambda g: [plane(coarse_sol, 8 * g + m) for m in range(8)]), 0, unroll=True)

    put(face, 0, rows(out_sol, 64, 64))
    put(face, 64, rows(out_sol, 32 * 64, 64))
    for axis, parity in enumerate(parities(blk)):
        for color in range(2):
            d = 2 * axis + (parity == color).astype(jnp.int32)
            out[ORDER.index(2 * axis + color)][...] = rows(face, d * 64, 64)


def residual_kernel(level, parent, neighbor, src, sol, *refs):
    sent, got = ([refs[first + ORDER.index(n)] for n in range(6)] for first in (0, 6))
    last, fine = level is None, level == 0
    if fine:
        res, nxt, own, halo, table, down = refs[12:]
    elif last:
        out, halo, table, res, given, sems = refs[12:]
    else:
        res, halo, table = refs[12:]
    sec, blk = position()

    def whole():
        j, k = lane_parts()

        for axis, parity in enumerate(parities(blk)):
            for color in range(2):
                odd = (parity == color).astype(jnp.int32)
                put(table, (2 * axis + 1 - odd) * 128, sent[2 * axis + color][...])
                put(table, (2 * axis + odd) * 128 + 64, got[2 * axis + color][...])
        device = sec * N_BLK + blk

        def gather(g, _):
            for d in range(6):
                other = neighbor[g, d]
                local = (other >> 3) == device
                start = d * 128 + jnp.where(local, 0, 64) + (other & 7)
                value = table[pl.ds(start, 8, stride=8), :]
                halo[pl.ds(d * 64 + g, 8, stride=8), :] = jnp.where(other >= 0, value, 0.0)
            return 0

        lax.fori_loop(0, FAM, gather, 0)

        def side(base):
            return [[rows(halo, base + (q * 2 + o) * 8) for o in range(2)] for q in range(4)]

        def residue(x, a, below, above):
            y_at, z_at = x & 7, x & 15
            y_rows = [128 + (o * 4 + (x >> 3)) * 8 for o in range(2)]
            hy = [
                [roll(rows(halo, y_rows[o]), (128 - 16 * y_at) & 127) for o in range(2)],
                [roll(rows(halo, y_rows[o] + 64), 112 - 16 * y_at) for o in range(2)],
            ]
            hz = []
            for q in range(4):
                at = 256 + (q * 2 + (x >> 4)) * 8
                hz.append([roll(rows(halo, at), (128 - z_at) & 127), roll(rows(halo, at + 64), 15 - z_at)])
            m = around(a, below, above, j, k, hy, hz)
            s = plane(src, x)
            return [[s[q][o] - 6.0 * a[q][o] + m[q][o] for o in range(2)] for q in range(4)]

        def group(x):
            p = [side(0) if x == 0 else plane(sol, x - 1)]
            p += [plane(sol, x + m) for m in range(RESIDUE)]
            p.append(side(64) if x + RESIDUE == 32 else plane(sol, x + RESIDUE))
            r = [residue(x + m, p[m + 1], p[m], p[m + 2]) for m in range(RESIDUE)]
            for m in range(RESIDUE):
                put_plane(res, x + m, r[m])
            if fine:
                for m in range(0, RESIDUE, 2):
                    put_down(down, (x + m) // 2, restrict_pair(r[m], r[m + 1]))

        for half in range(2):
            for x in range(8 * half, 32, 16):
                for first in range(x, x + 8, RESIDUE):
                    group(first)
            if last:
                unload_half(res, given, out, sems, half)
        if last:
            finish_unload(given, out, sems)
        if fine:
            send_down(down, parent, blk, own, nxt, False)

    if last:
        whole()
    else:
        pl.when(sec == level)(whole)


def fine_kernel(res, sol, out_sol, rhs, mid):
    sec, _ = position()

    @pl.when(sec == 0)
    def _():
        def copy(i, _):
            put(rhs, i * 64, rows(res, i * 64, 64))
            return 0

        lax.fori_loop(1, 33, copy, 0)

        def emit(at, value):
            put(out_sol, at, rows(sol, at) + value)

        smooth(rhs, mid, emit)


def unload_kernel(sol, out, given, sems):
    for half in range(2):
        unload_half(sol, given, out, sems, half)
    finish_unload(given, out, sems)


def shape(n, dtype=F32):
    return jax.ShapeDtypeStruct((n, 128), dtype)


def scratch(n):
    return pltpu.VMEM((n, 128), F32)


def call(kernel, name, in_specs, out_shape, scratch_shapes=(), out_specs=None):
    return pl.pallas_call(
        kernel,
        name=name,
        in_specs=in_specs,
        out_shape=out_shape,
        out_specs=out_specs or [VMEM] * len(out_shape),
        scratch_shapes=list(scratch_shapes),
        compiler_params=pltpu.CompilerParams(vmem_limit_bytes=32 << 20),
    )


def local(source, parent, neighbor):
    tiles = source.reshape(FAM, 8, 32, 128).transpose(0, 2, 1, 3).reshape(2048, 128)
    here = pltpu.with_memory_space_constraint(tiles, pltpu.HBM)
    place = pltpu.with_memory_space_constraint(parent, pltpu.HBM)
    pad, pads = shape(PAD_ROWS), scratch(PAD_ROWS)

    def both(nxt, own, pairs):
        return swap(nxt, pairs), swap(own, OWN_PAIRS)

    nxt, own = call(
        first_down_kernel,
        "first_down",
        [HBM, HBM],
        (shape(136), shape(136)),
        [
            scratch(256),
            scratch(2048),
            pltpu.SMEM((FAM,), jnp.int32),
            pltpu.SemaphoreType.DMA((2, FAM)),
            pltpu.SemaphoreType.DMA,
        ],
    )(place, here)
    got_next, got_own = both(nxt, own, DOWN_PAIRS)
    src, fine_sol = call(load_kernel, "load", [VMEM], (pad, pad), [pads])(tiles)
    coarse_sol, nxt, own, tags = call(
        functools.partial(coarse_kernel, True),
        "coarse_0",
        [VMEM] * 3,
        (pad, shape(128), shape(128), jax.ShapeDtypeStruct((8,), jnp.int32)),
        [pads, pads, pltpu.SMEM((2, 8, 128), F32), pltpu.SemaphoreType.DMA((2,))],
        [VMEM, VMEM, VMEM, SMEM],
    )(src, got_next, got_own)

    def lift_and_share(n, nxt, own):
        got_next, got_own = both(nxt, own, UP_PAIRS)
        out = call(
            lift_kernel,
            f"lift_{n}",
            [SMEM] + [VMEM] * 4,
            (pad,) + (shape(64),) * 6,
            [scratch(256), scratch(384)],
        )(parent, fine_sol, coarse_sol, got_next, got_own)
        sol, sent = out[0], out[1:]
        return sol, [*sent, *(swap(face, HALO_PAIRS[n]) for face, n in zip(sent, ORDER))]

    def residue_of(level, name, sol, faces, out_shape, more=(), out_specs=None):
        return call(
            functools.partial(residual_kernel, level),
            name,
            [SMEM, SMEM] + [VMEM] * 14,
            out_shape,
            [scratch(384), scratch(768), *more],
            out_specs,
        )(parent, neighbor, src, sol, *faces)

    sol, faces = lift_and_share(0, nxt, own)
    res, nxt, own = residue_of(0, "residue_fine", sol, faces, (pad, shape(128), shape(128)), [scratch(256)])
    got_next, got_own = both(nxt, own, DOWN_PAIRS)
    (coarse_res,) = residue_of(1, "residue_coarse", sol, faces, (pad,))
    (fine_sol,) = call(fine_kernel, "fine", [VMEM, VMEM], (pad,), [pads, pads])(res, sol)
    coarse_sol, nxt, own = call(
        functools.partial(coarse_kernel, False),
        "coarse_1",
        [SMEM] + [VMEM] * 5,
        (pad, shape(128), shape(128)),
        [pads, pads, pads],
    )(tags, coarse_res, sol, fine_sol, got_next, got_own)
    sol, faces = lift_and_share(1, nxt, own)
    leave = [scratch(2048), pltpu.SemaphoreType.DMA((2, FAM))]
    (solution,) = call(unload_kernel, "unload", [VMEM], (shape(2048),), leave, [HBM])(sol)
    (residual,) = residue_of(None, "residual", sol, faces, (shape(2048),), [pads, *leave], [HBM])

    def blocks(x):
        return x.reshape(FAM, 32, 8, 128).transpose(0, 2, 1, 3).reshape(64, 4096)

    return blocks(solution), blocks(residual)


def solution(mesh):
    return jax.shard_map(
        local,
        mesh=mesh,
        in_specs=(P(AX, None), P(AX), P(AX, None)),
        out_specs=(P(AX, None), P(AX, None)),
        check_vma=False,
    )
```
